32 devices in a mesh: slab: 32 (over z, y, x, core).
Axes of the slice: x: 2, y: 2, z: 4, core: 2. Of those that a mesh axis runs over, the one named last changes fastest.
Arguments:
- diag_tiles: float32 [128, 256, 256], P('slab'), may hold values from 0 to 1, as said below
- coupling: float32 [128, 256, 256], P('slab'), may hold values from 0 to 1, as said below
- labels: int32 [32768], P('slab'), may hold values from 0 to 511
- confidence: float32 [32768], P('slab'), may hold values from 0.25 to 4
Outputs:
- propagated: float32 [32768, 512], P('slab')
The draws below stay inside these ranges and needn't reach their ends.
Inputs may be any that keep to these rules, and one draw needn't show every extreme that they name: diag_tiles[i] is symmetric with a zero diagonal and non-negative entries; the symmetric matrix with blocks diag_tiles[i] on the diagonal, coupling[i] below it and its transpose above it (i >= 1) has spectral radius at most 1. `coupling`: all entries are non-negative.
All inputs are finite; a program needn't handle non-finite values.
Results may differ from the reference program's by a relative error of at most 0.0003.
Values sent between devices are 32-bit elements; how exact they have to be, the bound alone decides.
No kernel may reach another device: no remote copies, remote signals or barrier semaphores. Data moves between devices by JAX's collectives and lax.ppermute only.
A program may use at most 128 MiB of HBM per device.

```python
import math
import jax
import jax.numpy as jnp
from jax import lax

B = 256
C = 512
NB = 128
ROWS = 32768


def draw_weights(key, shape):
    return jnp.exp(jax.random.uniform(key, shape, jnp.float32, math.log(0.1), 0.0))


def build_graph(key):
    count = 6
    inner_factor = 0.1
    key_diag_shift = jax.random.fold_in(key, 11)
    key_diag_weight = jax.random.fold_in(key, 12)
    key_link_shift = jax.random.fold_in(key, 13)
    key_link_weight = jax.random.fold_in(key, 14)
    diag_shift = jax.random.randint(key_diag_shift, (NB, count), 1, 4)
    link_shift = (jax.random.randint(key_link_shift, (NB, count), -1, 2) + B) % B
    diag_weight = inner_factor * draw_weights(key_diag_weight, (NB, count, B))
    link_weight = draw_weights(key_link_weight, (NB, count, B))
    positions = jnp.arange(B, dtype=jnp.int32)
    block_ids = jnp.arange(NB, dtype=jnp.int32)
    diag_raw = jnp.zeros((NB, B, B), jnp.float32)
    link_raw = jnp.zeros((NB, B, B), jnp.float32)
    diag_degree = jnp.zeros((NB, B), jnp.float32)
    link_rows = jnp.zeros((NB, B), jnp.float32)
    link_cols = jnp.zeros((NB, B), jnp.float32)
    for index in range(count):
        shift = diag_shift[:, index][:, None]
        weight = diag_weight[:, index, :]
        target = (positions[None, :] + shift) % B
        placed = jnp.where(target[:, :, None] == positions[None, None, :], weight[:, :, None], 0.0)
        diag_raw = diag_raw + placed + jnp.swapaxes(placed, 1, 2)
        source = (positions[None, :] - shift) % B
        diag_degree = diag_degree + weight + jnp.take_along_axis(weight, source, axis=1)
        link_step = link_shift[:, index][:, None]
        link_value = link_weight[:, index, :]
        link_target = (positions[None, :] + link_step) % B
        link_raw = link_raw + jnp.where(link_target[:, :, None] == positions[None, None, :], link_value[:, :, None], 0.0)
        link_rows = link_rows + link_value
        link_source = (positions[None, :] - link_step) % B
        link_cols = link_cols + jnp.take_along_axis(link_value, link_source, axis=1)
    row_part = jnp.where((block_ids >= 1)[:, None], link_rows, 0.0)
    col_part = jnp.where((block_ids <= NB - 2)[:, None], jnp.roll(link_cols, -1, axis=0), 0.0)
    degree = diag_degree + row_part + col_part
    root = jnp.sqrt(degree)
    diag_tiles = diag_raw / (root[:, :, None] * root[:, None, :])
    prev_root = jnp.roll(root, 1, axis=0)
    edge_scale = jnp.where(block_ids == 0, 0.5, 1.0)[:, None, None]
    coupling = edge_scale * link_raw / (root[:, :, None] * prev_root[:, None, :])
    return (diag_tiles.astype(jnp.float32), coupling.astype(jnp.float32))


def draw_diag_tiles(key, part):
    diag_tiles, coupling = build_graph(key)
    return diag_tiles


def draw_coupling(key, part):
    diag_tiles, coupling = build_graph(key)
    return coupling


def plant(array, stream_key, least, largest):
    longest = array.shape.index(max(array.shape))
    spots = []
    for shift in (0, 1):
        where = [jax.random.randint(jax.random.fold_in(stream_key, axis), (), 0, length) for axis, length in enumerate(array.shape)]
        where[longest] = (where[longest] + shift) % array.shape[longest]
        spots.append(tuple(where))
    return array.at[spots[0]].set(least).at[spots[1]].set(largest)


def levels(stream_key, dims, cuts, low, high):
    loudness = 1.0
    for position, blocks in cuts:
        heights = jax.random.uniform(jax.random.fold_in(jax.random.fold_in(stream_key, 6), position), (blocks,), jnp.float32, low / len(cuts), high / len(cuts))
        loudness = loudness * jnp.repeat(jnp.exp(heights), dims[position] // blocks).reshape((-1,) + (1,) * (len(dims) - 1 - position))
    return loudness


def setup_inputs(seed: int = 0) -> dict:
    key_of = jax.random.split(jax.random.key(seed), 5)
    diag_tiles = draw_diag_tiles(jax.random.fold_in(key_of[4], 71), 0)
    coupling = draw_coupling(jax.random.fold_in(key_of[4], 71), 0)
    labels = plant(jax.random.randint(key_of[2], (ROWS,), 0, C), jax.random.fold_in(key_of[2], 1), 0, C - 1).astype(jnp.int32)
    confidence = jnp.clip(jnp.exp(math.log(4.0) - 2.7725887 * jax.random.uniform(key_of[3], (ROWS,), jnp.float32) ** levels(key_of[3], (ROWS,), ((0, 32),), -0.2, 0.2)), 0.25, 4.0)
    return {"diag_tiles": diag_tiles, "coupling": coupling, "labels": labels, "confidence": confidence}


alpha_rate = 0.995

def product(left, right):
    return jnp.dot(left.astype(jnp.float32), right.astype(jnp.float32), precision=lax.Precision.HIGHEST, preferred_element_type=jnp.float32)

def reference(diag_tiles, coupling, labels, confidence):
    identity = jnp.eye(B, dtype=jnp.float32)
    diag_ops = identity[None] - alpha_rate * diag_tiles
    left_ops = (-alpha_rate * coupling).at[0].set(0.0)
    seeds = jnp.where(labels[:, None] == jnp.arange(C)[None, :], confidence[:, None], 0.0).astype(jnp.float32)
    sources = seeds.reshape(NB, B, C)

    def forward(carry, item):
        last_factor, last_solved = carry
        block_diag, block_link, block_rhs = item
        linked = jax.scipy.linalg.solve_triangular(last_factor, block_link.T, lower=True)
        factor = jnp.linalg.cholesky(block_diag - product(linked.T, linked))
        solved = jax.scipy.linalg.solve_triangular(factor, block_rhs - product(linked.T, last_solved), lower=True)
        return ((factor, solved), (factor, solved, linked))
    start = (identity, jnp.zeros((B, C), jnp.float32))
    _, (factors, solveds, linkeds) = lax.scan(forward, start, (diag_ops, left_ops, sources))
    next_linked = jnp.concatenate([linkeds[1:], jnp.zeros((1, B, B), jnp.float32)], axis=0)

    def backward(later, item):
        factor, solved, linked = item
        current = jax.scipy.linalg.solve_triangular(factor, solved - product(linked, later), lower=True, trans=1)
        return (current, current)
    _, values = lax.scan(backward, jnp.zeros((B, C), jnp.float32), (factors, solveds, next_linked), reverse=True)
    return values.reshape(ROWS, C)
```

```python
import functools

import jax
import jax.numpy as jnp
from jax import lax
from jax.experimental import pallas as pl
from jax.experimental.pallas import tpu as pltpu
from jax.sharding import PartitionSpec as P

C = 512

alpha_rate = 0.995

f32 = jnp.float32
bf16 = jnp.bfloat16

NN = (((1,), (0,)), ((), ()))
NT = (((1,), (1,)), ((), ()))
TN = (((0,), (0,)), ((), ()))


def product(left, right, dims=NN):
    return lax.dot_general(left, right, dims, precision=lax.Precision.HIGHEST, preferred_element_type=f32)


def single(left, right, dims=NN):
    return lax.dot_general(left, right, dims, preferred_element_type=f32)


def halves(array):
    high = array.astype(bf16)
    return high, (array - high.astype(f32)).astype(bf16)


def product3(left, right, dims=NN):
    left_high, left_low = halves(left)
    right_high, right_low = halves(right)
    return single(left_high, right_high, dims) + (
        single(left_high, right_low, dims) + single(left_low, right_high, dims)
    )


def unit(width):
    rows = lax.broadcasted_iota(jnp.int32, (width, width), 0)
    columns = lax.broadcasted_iota(jnp.int32, (width, width), 1)
    return (rows == columns).astype(f32)


DOUBLINGS = 6


def inverses(matrices):
    width = matrices[0].shape[0]
    identity = unit(width)
    scale = 1.0 / alpha_rate
    residuals = [identity - matrix for matrix in matrices]
    results = [identity for _ in matrices]
    for step in range(DOUBLINGS):
        following = 2.0 * scale * scale - 1.0
        gain = 2.0 * scale * scale / following
        next_residuals, next_results = [], []
        for residual, result in zip(residuals, results):
            if step == 0:
                next_residuals.append(gain * product3(residual, residual) - identity * (1.0 / following))
                next_results.append(gain * (identity + residual))
            elif step < DOUBLINGS - 1:
                both = product3(jnp.concatenate([residual, result], axis=0), residual)
                next_residuals.append(gain * both[:width] - identity * (1.0 / following))
                next_results.append(gain * (result + both[width:]))
            else:
                next_residuals.append(residual)
                next_results.append(gain * (result + product3(result, residual)))
        residuals, results = next_residuals, next_results
        scale = following
    for multiply in (product3, product):
        errors = [identity - multiply(matrix, result) for matrix, result in zip(matrices, results)]
        results = [result + multiply(result, error) for result, error in zip(results, errors)]
    return results


def call(kernel, shapes, operands, microseconds, scratch=(), flags=True):
    in_specs = [pl.BlockSpec(memory_space=pltpu.VMEM) for _ in operands]
    if flags:
        in_specs[0] = pl.BlockSpec(memory_space=pltpu.SMEM)
    return pl.pallas_call(
        kernel,
        out_shape=[jax.ShapeDtypeStruct(shape, f32) for shape in shapes],
        in_specs=in_specs,
        out_specs=[pl.BlockSpec(memory_space=pltpu.VMEM) for _ in shapes],
        scratch_shapes=[pltpu.VMEM(shape, f32) for shape in scratch],
        cost_estimate=pl.CostEstimate(flops=int(microseconds * 1.1e9), bytes_accessed=0, transcendentals=0),
        compiler_params=pltpu.CompilerParams(vmem_limit_bytes=40 * 2**20),
    )(*operands)


def join_rows(target, mine, other, core):
    half = mine.shape[-2]
    target[..., pl.ds(pl.multiple_of(core * half, half), half), :] = mine[...]
    target[..., pl.ds(pl.multiple_of((1 - core) * half, half), half), :] = other[...]


def local_factor(flags, diag, coupling, inverse_out, link_out, crit, rest, *, width):
    identity = unit(width)
    d = [identity - alpha_rate * diag[i] for i in range(4)]
    l = [-alpha_rate * coupling[i] for i in range(4)]
    l[0] = jnp.where(flags[1] == 1, 0.0, l[0])
    v0, v2 = inverses([d[0], d[2]])
    v0_l1t = product(v0, l[1], NT)
    v2_l2 = product(v2, l[2])
    middle = d[1] - product(l[1], v0_l1t) - product(l[2], v2_l2, TN)
    (v1,) = inverses([middle])
    v0_l0 = product(v0, l[0])
    v2_l3t = product(v2, l[3], NT)
    g = -product(l[1], v0_l0)
    h = -product(l[2], v2_l3t, TN)
    v1_g = product(v1, g)
    v1_h = product(v1, h)
    left = -product(l[0], v0_l0, TN) - product(g, v1_g, TN)
    right = d[3] - product(l[3], v2_l3t) - product(h, v1_h, TN)
    across = -product(g, v1_h, TN)
    crit[...] = jnp.where(flags[2] == 0, right, left)
    rest[0] = jnp.where(flags[2] == 0, left, right)
    rest[1] = across
    inverse_out[0] = v0
    inverse_out[1] = v1
    inverse_out[2] = v2
    for i, value in enumerate((v0_l0, v0_l1t, v1_g, v1_h, v2_l2, v2_l3t)):
        link_out[i] = value


def local_sides(flags, labels, confidence, inverse, link, keep, send, interior, *, width, classes):
    place = lax.broadcasted_iota(jnp.int32, (width, classes), 1)
    b = []
    for i in range(4):
        b.append(jnp.where(labels[i] == place, confidence[i], 0.0))
    b1 = b[1] - product(link[1], b[0], TN) - product(link[4], b[2], TN)
    left = -product(link[0], b[0], TN) - product(link[2], b1, TN)
    right = b[3] - product(link[5], b[2], TN) - product(link[3], b1, TN)
    y1 = product(inverse[1], b1)
    y0 = product(inverse[0], b[0]) - product(link[1], y1)
    y2 = product(inverse[2], b[2]) - product(link[4], y1)
    interior[0] = y0
    interior[1] = y1
    interior[2] = y2
    lower = flags[0] == 0
    half = classes // 2
    crit = jnp.where(lower, right, left)
    rest = jnp.where(lower, left, right)
    keep[0] = jnp.where(lower, crit[:, :half], crit[:, half:])
    keep[1] = jnp.where(lower, rest[:, :half], rest[:, half:])
    send[0] = jnp.where(lower, crit[:, half:], crit[:, :half])
    send[1] = jnp.where(lower, rest[:, half:], rest[:, :half])


def local_spikes(flags, link, spikes, *, width):
    s1 = jnp.concatenate([link[2], link[3]], axis=1)
    spikes[1] = s1
    first = -product(link[1], s1)
    spikes[0, :, :width] = first[:, :width] + link[0]
    spikes[0, :, width:] = first[:, width:]
    last = -product(link[4], s1)
    spikes[2, :, :width] = last[:, :width]
    spikes[2, :, width:] = last[:, width:] + link[5]


def level_inverse(flags, *refs, halved):
    if halved:
        crit, mine, other, out, whole = refs
        join_rows(whole, mine, other, flags[0])
        received = whole[...]
    else:
        crit, mine, out = refs
        received = mine[...]
    (inverse,) = inverses([crit[...] + received])
    out[...] = inverse


def level_merge(flags, *refs, halved, level, final):
    if halved:
        inverse, rest, mine, other, back, crit_out, rest_out, crit_half, rest_half, whole = refs
        join_rows(whole, mine, other, flags[0])
        received = whole
    else:
        inverse, rest, mine, back, crit_out, rest_out, crit_half, rest_half = refs
        received = mine
    lower = flags[2 + level] == 0
    a_left = jnp.where(lower, rest[0], received[0])
    b_left = jnp.where(lower, rest[1], received[1])
    c_right = jnp.where(lower, received[0], rest[0])
    b_right = jnp.where(lower, received[1], rest[1])
    to_left = product(inverse[...], b_left, NT)
    to_right = product(inverse[...], b_right)
    left = a_left - product(b_left, to_left)
    right = c_right - product(b_right, to_right, TN)
    rest_out[1] = -product(b_left, to_right)
    next_lower = final | (flags[3 + level] == 0)
    crit_out[...] = jnp.where(next_lower, right, left)
    rest_out[0] = jnp.where(next_lower, left, right)
    back[0] = to_left
    back[1] = to_right
    half = crit_half.shape[0]
    rows = pl.ds(pl.multiple_of(flags[0] * half, half), half)
    crit_half[...] = crit_out[rows, :]
    rest_half[...] = rest_out[:, rows, :]


def level_sides(flags, inverse, back, own, received, value, out, *, level, final):
    lower = flags[2 + level] == 0
    g = own[0] + received[0]
    a_left = jnp.where(lower, own[1], received[1])
    c_right = jnp.where(lower, received[1], own[1])
    value[...] = product(inverse[...], g)
    left = a_left - product(back[0], g, TN)
    right = c_right - product(back[1], g, TN)
    next_lower = final | (flags[3 + level] == 0)
    out[0] = jnp.where(next_lower, right, left)
    out[1] = jnp.where(next_lower, left, right)


def end_factor(flags, crit, rest, end, across, crit_out, crit_half, *, level):
    (inverse,) = inverses([crit[...]])
    end[...] = inverse
    scaled = product(rest[1], inverse)
    across[...] = scaled
    crit_out[...] = jnp.where(flags[2 + level] == 0, crit[...], rest[0] - product(scaled, rest[1], NT))
    half = crit_half.shape[0]
    crit_half[...] = crit_out[pl.ds(pl.multiple_of(flags[0] * half, half), half), :]


def end_sides(flags, across, own, out, *, level):
    out[...] = jnp.where(flags[2 + level] == 0, own[0], own[1] - product(across[...], own[0]))


def descend(flags, *refs, levels):
    root, own, received, end, across, sides = refs[:6]
    backs = refs[6 : 6 + levels - 1]
    values = refs[6 + levels - 1 : 6 + 2 * (levels - 1)]
    keep, send = refs[-2:]
    lower = flags[2 + levels - 1] == 0
    q = product(root[...], own[...] + received[...])
    far = product(end[...], sides[0]) - product(across[...], q, TN)
    p = jnp.where(lower, 0.0, q)
    r = jnp.where(lower, q, far)
    for level in range(levels - 2, -1, -1):
        q = values[level][...] - product(backs[level][0], p) - product(backs[level][1], r)
        if level:
            lower = flags[2 + level] == 0
            p, r = jnp.where(lower, p, q), jnp.where(lower, q, r)
    lower = flags[0] == 0
    keep[0] = jnp.where(lower, p, q)
    keep[1] = jnp.where(lower, q, r)
    send[0] = jnp.where(lower, q, p)
    send[1] = jnp.where(lower, r, q)


def finish(flags, keep, received, spikes, interior, out, ends, *, width, classes):
    half = classes // 2
    lower = flags[0] == 0
    for i in range(2):
        ends[i * width : (i + 1) * width, :half] = jnp.where(lower, keep[i], received[i])
        ends[i * width : (i + 1) * width, half:] = jnp.where(lower, received[i], keep[i])
    for i in range(3):
        out[i * width : (i + 1) * width, :] = interior[i] - product(spikes[i], ends[...])
    out[3 * width :, :] = ends[width:, :]


def swapped(array, distance):
    length = lax.axis_size("slab")
    return lax.ppermute(array, "slab", [(i, i ^ distance) for i in range(length)])


def shards(diag_tiles, coupling, labels, confidence):
    blocks, width, _ = diag_tiles.shape
    classes = C
    square, half, pair, half_pair = (width, width), (width // 2, width), (2, width, width), (2, width // 2, width)
    cols = (width, classes // 2)
    col_pair = (2,) + cols
    levels = lax.axis_size("slab").bit_length() - 1
    position = lax.axis_index("slab")
    flags = jnp.stack(
        [position & 1, (position == 0).astype(jnp.int32)] + [(position >> k) & 1 for k in range(levels)] + [position * 0]
    )
    inverse, link, crit, rest = call(
        functools.partial(local_factor, width=width),
        [(3,) + square, (6,) + square, square, pair],
        [flags, diag_tiles, coupling],
        16,
    )
    received = swapped(crit, 1)
    received_rest = swapped(rest, 1)
    keep, send, interior = call(
        functools.partial(local_sides, width=width, classes=classes),
        [col_pair, col_pair, (3, width, classes)],
        [flags, labels.reshape(blocks, width, 1), confidence.reshape(blocks, width, 1), inverse, link],
        6,
    )
    received_sides = swapped(send, 1)
    sides = keep
    (spikes,) = call(functools.partial(local_spikes, width=width), [(3, width, 2 * width)], [flags, link], 2)
    incoming, incoming_rest = [received], [received_rest]
    backs, values = [], []
    for level in range(levels - 1):
        halved = level > 0
        (middle,) = call(
            functools.partial(level_inverse, halved=halved), [square], [flags, crit] + incoming, 4, [square] * halved
        )
        back, crit, rest, crit_half, rest_half = call(
            functools.partial(level_merge, halved=halved, level=level, final=level == levels - 2),
            [pair, square, pair, half, half_pair],
            [flags, middle, rest] + incoming_rest,
            3,
            [pair] * halved,
        )
        if level + 1 < levels - 1:
            arrived = swapped(crit_half, 2 ** (level + 1))
            incoming = [arrived, swapped(arrived, 1)]
            arrived = swapped(rest_half, 2 ** (level + 1))
            incoming_rest = [arrived, swapped(arrived, 1)]
        value, sides = call(
            functools.partial(level_sides, level=level, final=level == levels - 2),
            [cols, col_pair],
            [flags, middle, back, sides, received_sides],
            2,
        )
        if level + 1 < levels - 1:
            received_sides = swapped(sides, 2 ** (level + 1))
        backs.append(back)
        values.append(value)
    last = levels - 1
    end, across, crit, crit_half = call(
        functools.partial(end_factor, level=last), [square, square, square, half], [flags, crit, rest], 6
    )
    arrived = swapped(crit_half, 2**last)
    other = swapped(arrived, 1)
    (own,) = call(functools.partial(end_sides, level=last), [cols], [flags, across, sides], 1)
    received_own = swapped(own, 2**last)
    (root,) = call(functools.partial(level_inverse, halved=True), [square], [flags, crit, arrived, other], 4, [square])
    keep, send = call(
        functools.partial(descend, levels=levels),
        [col_pair, col_pair],
        [flags, root, own, received_own, end, across, sides] + backs + values,
        5,
    )
    received = swapped(send, 1)
    (out,) = call(
        functools.partial(finish, width=width, classes=classes),
        [(blocks * width, classes)],
        [flags, keep, received, spikes, interior],
        4,
        [(2 * width, classes)],
    )
    return out


def solution(mesh):
    in_specs = (P("slab", None, None), P("slab", None, None), P("slab"), P("slab"))
    out_specs = P("slab", None)
    return jax.shard_map(shards, mesh=mesh, in_specs=in_specs, out_specs=out_specs, check_vma=False)
```

```python
import functools

import jax
import jax.numpy as jnp
from jax import lax
from jax.experimental import pallas as pl
from jax.experimental.pallas import tpu as pltpu
from jax.sharding import PartitionSpec as P

C = 512

alpha_rate = 0.995

f32 = jnp.float32
bf16 = jnp.bfloat16

NN = (((1,), (0,)), ((), ()))
NT = (((1,), (1,)), ((), ()))
TN = (((0,), (0,)), ((), ()))


def product(left, right, dims=NN):
    return lax.dot_general(left, right, dims, precision=lax.Precision.HIGHEST, preferred_element_type=f32)


def single(left, right, dims=NN):
    return lax.dot_general(left, right, dims, preferred_element_type=f32)


def halves(array):
    high = array.astype(bf16)
    return high, (array - high.astype(f32)).astype(bf16)


def product3(left, right, dims=NN):
    left_high, left_low = halves(left)
    right_high, right_low = halves(right)
    return single(left_high, right_high, dims) + (
        single(left_high, right_low, dims) + single(left_low, right_high, dims)
    )


def unit(width):
    rows = lax.broadcasted_iota(jnp.int32, (width, width), 0)
    columns = lax.broadcasted_iota(jnp.int32, (width, width), 1)
    return (rows == columns).astype(f32)


DOUBLINGS = 6


def inverses(matrices):
    width = matrices[0].shape[0]
    identity = unit(width)
    scale = 1.0 / alpha_rate
    residuals = [identity - matrix for matrix in matrices]
    results = [identity for _ in matrices]
    for step in range(DOUBLINGS):
        following = 2.0 * scale * scale - 1.0
        gain = 2.0 * scale * scale / following
        next_residuals, next_results = [], []
        for residual, result in zip(residuals, results):
            if step == 0:
                next_residuals.append(gain * product3(residual, residual) - identity * (1.0 / following))
                next_results.append(gain * (identity + residual))
            elif step < DOUBLINGS - 1:
                both = product3(jnp.concatenate([residual, result], axis=0), residual)
                next_residuals.append(gain * both[:width] - identity * (1.0 / following))
                next_results.append(gain * (result + both[width:]))
            else:
                next_residuals.append(residual)
                next_results.append(gain * (result + product3(result, residual)))
        residuals, results = next_residuals, next_results
        scale = following
    for multiply in (product3, product):
        errors = [identity - multiply(matrix, result) for matrix, result in zip(matrices, results)]
        results = [result + multiply(result, error) for result, error in zip(results, errors)]
    return results


def call(kernel, shapes, operands, microseconds, scratch=(), hbm=(), out_hbm=False):
    in_specs = [pl.BlockSpec(memory_space=pltpu.VMEM) for _ in operands]
    in_specs[0] = pl.BlockSpec(memory_space=pltpu.SMEM)
    for index in hbm:
        in_specs[index] = pl.BlockSpec(memory_space=pl.ANY)
    return pl.pallas_call(
        kernel,
        out_shape=[jax.ShapeDtypeStruct(shape, f32) for shape in shapes],
        in_specs=in_specs,
        out_specs=[pl.BlockSpec(memory_space=pl.ANY if out_hbm else pltpu.VMEM) for _ in shapes],
        scratch_shapes=[pltpu.VMEM(shape, f32) if isinstance(shape, tuple) else shape for shape in scratch],
        cost_estimate=pl.CostEstimate(flops=int(microseconds * 1.1e9), bytes_accessed=0, transcendentals=0),
        compiler_params=pltpu.CompilerParams(vmem_limit_bytes=40 * 2**20),
    )(*operands)


def join_rows(target, mine, other, core):
    half = mine.shape[-2]
    target[..., pl.ds(pl.multiple_of(core * half, half), half), :] = mine[...]
    target[..., pl.ds(pl.multiple_of((1 - core) * half, half), half), :] = other[...]


def pack(matrix, out):
    half = matrix.shape[0] // 2
    rows = lax.broadcasted_iota(jnp.int32, (half, half), 0)
    columns = lax.broadcasted_iota(jnp.int32, (half, half), 1)
    last = matrix[half:, half:]
    out[:half, :half] = matrix[half:, :half]
    out[:half, half:] = jnp.where(rows >= columns, matrix[:half, :half], last)
    diagonal = jnp.sum(jnp.where(rows == columns, last, 0.0), axis=0, keepdims=True)
    out[half:, half:] = jnp.broadcast_to(diagonal, (8, half))
    out[half:, :half] = jnp.zeros((8, half), f32)


def unpack(packed):
    half = packed.shape[1] // 2
    rows = lax.broadcasted_iota(jnp.int32, (half, half), 0)
    columns = lax.broadcasted_iota(jnp.int32, (half, half), 1)
    corner = packed[:half, :half]
    both = packed[:half, half:]
    flipped = both.T
    diagonal = packed[half : half + 1, half:]
    first = jnp.where(rows >= columns, both, flipped)
    last = jnp.where(rows < columns, both, jnp.where(rows > columns, flipped, diagonal))
    return jnp.concatenate(
        [jnp.concatenate([first, corner.T], axis=1), jnp.concatenate([corner, last], axis=1)], axis=0
    )


def local_factor(flags, diag_in, coupling_in, inverse_out, link_out, crit, rest, diag, coupling, sems, *, width):
    copies = []
    for i in (0, 2, 1, 3):
        copies.append(pltpu.make_async_copy(diag_in.at[i], diag.at[i], sems.at[i]))
    for i in range(4):
        copies.append(pltpu.make_async_copy(coupling_in.at[i], coupling.at[i], sems.at[4 + i]))
    for copy in copies:
        copy.start()
    identity = unit(width)
    copies[0].wait()
    copies[1].wait()
    v0, v2 = inverses([identity - alpha_rate * diag[0], identity - alpha_rate * diag[2]])
    for copy in copies[2:]:
        copy.wait()
    d1 = identity - alpha_rate * diag[1]
    d3 = identity - alpha_rate * diag[3]
    l = [-alpha_rate * coupling[i] for i in range(4)]
    l[0] = jnp.where(flags[1] == 1, 0.0, l[0])
    v0_l1t = product(v0, l[1], NT)
    v2_l2 = product(v2, l[2])
    middle = d1 - product(l[1], v0_l1t) - product(l[2], v2_l2, TN)
    (v1,) = inverses([middle])
    v0_l0 = product(v0, l[0])
    v2_l3t = product(v2, l[3], NT)
    g = -product(l[1], v0_l0)
    h = -product(l[2], v2_l3t, TN)
    v1_g = product(v1, g)
    v1_h = product(v1, h)
    left = -product(l[0], v0_l0, TN) - product(g, v1_g, TN)
    right = d3 - product(l[3], v2_l3t) - product(h, v1_h, TN)
    across = -product(g, v1_h, TN)
    crit[...] = jnp.where(flags[2] == 0, right, left)
    rest[0] = jnp.where(flags[2] == 0, left, right)
    rest[1] = across
    inverse_out[0] = v0
    inverse_out[1] = v1
    inverse_out[2] = v2
    for i, value in enumerate((v0_l0, v0_l1t, v1_g, v1_h, v2_l2, v2_l3t, g, h)):
        link_out[i] = value


def local_sides(flags, seeds, inverse, link, keep, send, interior, *, width, classes):
    place = lax.broadcasted_iota(jnp.int32, (width, classes), 1).astype(f32)
    turned = seeds[...].T
    b = [jnp.where(turned[:, i : i + 1] == place, turned[:, 4 + i : 5 + i], 0.0) for i in range(4)]
    b1 = b[1] - product3(link[1], b[0], TN) - product3(link[4], b[2], TN)
    left = -product3(link[0], b[0], TN) - product3(link[2], b1, TN)
    right = b[3] - product3(link[5], b[2], TN) - product3(link[3], b1, TN)
    interior[0] = b[0]
    interior[1] = b1
    interior[2] = b[2]
    lower = flags[0] == 0
    half = classes // 2
    crit = jnp.where(lower, right, left)
    rest = jnp.where(lower, left, right)
    keep[0] = jnp.where(lower, crit[:, :half], crit[:, half:])
    keep[1] = jnp.where(lower, rest[:, :half], rest[:, half:])
    send[0] = jnp.where(lower, crit[:, half:], crit[:, :half])
    send[1] = jnp.where(lower, rest[:, half:], rest[:, :half])


def local_spikes(flags, inverse, link, sides, spikes, interior, *, width):
    y1 = product3(inverse[1], sides[1])
    interior[1] = y1
    interior[0] = product3(inverse[0], sides[0]) - product3(link[1], y1)
    interior[2] = product3(inverse[2], sides[2]) - product3(link[4], y1)
    s1 = jnp.concatenate([link[2], link[3]], axis=1)
    spikes[1] = s1
    first = -product3(link[1], s1)
    spikes[0, :, :width] = first[:, :width] + link[0]
    spikes[0, :, width:] = first[:, width:]
    last = -product3(link[4], s1)
    spikes[2, :, :width] = last[:, :width]
    spikes[2, :, width:] = last[:, width:] + link[5]


def level_inverse(flags, crit, received, out, *, packed):
    total = crit[...] + received[...]
    (inverse,) = inverses([unpack(total) if packed else total])
    out[...] = inverse


def level_merge(flags, *refs, halved, level, final):
    refs = list(refs)
    if halved:
        inverse, rest, mine, other = refs[:4]
        whole = refs.pop()
        outs = refs[4:]
        join_rows(whole, mine, other, flags[0])
        received = whole
    else:
        inverse, rest, received = refs[:3]
        outs = refs[3:]
    lower = flags[2 + level] == 0
    a_left = jnp.where(lower, rest[0], received[0])
    b_left = jnp.where(lower, rest[1], received[1])
    c_right = jnp.where(lower, received[0], rest[0])
    b_right = jnp.where(lower, received[1], rest[1])
    to_left = product(inverse[...], b_left, NT)
    to_right = product(inverse[...], b_right)
    left = a_left - product(b_left, to_left)
    right = c_right - product(b_right, to_right, TN)
    across = -product(b_left, to_right)
    back = outs[0]
    back[0] = to_left
    back[1] = to_right
    if final:
        crit_out, end, far = outs[1:]
        (inverse,) = inverses([right])
        end[...] = inverse
        scaled = product(across, inverse)
        far[...] = scaled
        pack(jnp.where(flags[3 + level] == 0, right, left - product(scaled, across, NT)), crit_out)
    else:
        crit_out, rest_out, rest_half = outs[1:]
        next_lower = flags[3 + level] == 0
        pack(jnp.where(next_lower, right, left), crit_out)
        rest_out[0] = jnp.where(next_lower, left, right)
        rest_out[1] = across
        half = rest_half.shape[1]
        rest_half[...] = rest_out[:, pl.ds(pl.multiple_of(flags[0] * half, half), half), :]


def level_sides(flags, inverse, back, own, received, *refs, level, split, final):
    lower = flags[2 + level] == 0
    g = own[0] + received[0]
    a_left = jnp.where(lower, own[1], received[1])
    c_right = jnp.where(lower, received[1], own[1])
    left = a_left - product3(back[0], g, TN)
    right = c_right - product3(back[1], g, TN)
    next_lower = flags[3 + level] == 0
    if final:
        far, value, out, ends = refs
        ends[...] = right
        out[...] = jnp.where(next_lower, right, left - product3(far[...], right))
    else:
        crit = jnp.where(next_lower, right, left)
        rest = jnp.where(next_lower, left, right)
        if split:
            value, keep, send = refs
            half = crit.shape[1] // 2
            for i, side in enumerate((crit, rest)):
                keep[i] = jnp.where(next_lower, side[:, :half], side[:, half:])
                send[i] = jnp.where(next_lower, side[:, half:], side[:, :half])
        else:
            value, out = refs
            out[0] = crit
            out[1] = rest
    value[...] = product3(inverse[...], g)


def descend(flags, *refs, levels):
    root, own, received, end, far, ends = refs[:6]
    count = levels - 2
    backs, values = refs[6 : 6 + count], refs[6 + count : 6 + 2 * count]
    keep, send = refs[-2:]
    lower = flags[2 + levels - 1] == 0
    q = product3(root[...], own[...] + received[...])
    outer = product3(end[...], ends[...]) - product3(far[...], q, TN)
    p = jnp.where(lower, 0.0, q)
    r = jnp.where(lower, q, outer)
    for level in range(levels - 2, 0, -1):
        q = values[level - 1][...] - product3(backs[level - 1][0], p) - product3(backs[level - 1][1], r)
        lower = flags[2 + level] == 0
        pair = (jnp.where(lower, p, q), jnp.where(lower, q, r))
        if level > 1:
            p, r = pair
    keep[0], keep[1] = pair
    send[0] = jnp.where(lower, q, p)
    send[1] = jnp.where(lower, r, q)


def descend_last(flags, mine, other, back, value, keep, send):
    lower = flags[3] == 0
    p, r = [
        jnp.concatenate([jnp.where(lower, mine[i], other[i]), jnp.where(lower, other[i], mine[i])], axis=1)
        for i in range(2)
    ]
    q = value[...] - product3(back[0], p) - product3(back[1], r)
    lower = flags[2] == 0
    keep[0] = jnp.where(lower, p, q)
    keep[1] = jnp.where(lower, q, r)
    send[0] = jnp.where(lower, q, p)
    send[1] = jnp.where(lower, r, q)


def finish(flags, keep, received, spikes, interior, out, ends, rows, sems, *, width, classes):
    half = classes // 2
    lower = flags[0] == 0
    for i in range(2):
        ends[i * width : (i + 1) * width, :half] = jnp.where(lower, keep[i], received[i])
        ends[i * width : (i + 1) * width, half:] = jnp.where(lower, received[i], keep[i])
    copies = [pltpu.make_async_copy(ends.at[pl.ds(width, width)], out.at[pl.ds(3 * width, width)], sems.at[3])]
    copies[0].start()
    for i in range(3):
        rows[i] = interior[i] - product3(spikes[i], ends[...])
        copies.append(pltpu.make_async_copy(rows.at[i], out.at[pl.ds(i * width, width)], sems.at[i]))
        copies[-1].start()
    for copy in copies:
        copy.wait()


def swapped(array, distance):
    length = lax.axis_size("slab")
    return lax.ppermute(array, "slab", [(i, i ^ distance) for i in range(length)])


def shards(diag_tiles, coupling, labels, confidence):
    blocks, width, _ = diag_tiles.shape
    classes = C
    square, pair, half_pair = (width, width), (2, width, width), (2, width // 2, width)
    packed = (width // 2 + 8, width)
    wide, narrow = (width, classes // 2), (width, classes // 4)
    levels = lax.axis_size("slab").bit_length() - 1
    position = lax.axis_index("slab")
    flags = jnp.stack([position & 1, (position == 0).astype(jnp.int32)] + [(position >> k) & 1 for k in range(levels)])
    seeds = jnp.concatenate([labels.reshape(blocks, width).astype(f32), confidence.reshape(blocks, width)], axis=0)
    inverse, link, crit, rest = call(
        functools.partial(local_factor, width=width),
        [(3,) + square, (8,) + square, square, pair],
        [flags, diag_tiles, coupling],
        13,
        [(4,) + square, (4,) + square, pltpu.SemaphoreType.DMA((8,))],
        (1, 2),
    )
    received_crit = swapped(crit, 1)
    received_rest = [swapped(rest, 1)]
    sides, send, inner = call(
        functools.partial(local_sides, width=width, classes=classes),
        [(2,) + wide, (2,) + wide, (3, width, classes)],
        [flags, seeds, inverse, link],
        3,
    )
    received_sides = swapped(send, 1)
    spikes, interior = call(
        functools.partial(local_spikes, width=width),
        [(3, width, 2 * width), (3, width, classes)],
        [flags, inverse, link, inner],
        3,
    )
    backs, values = [], []
    for level in range(levels - 1):
        final = level == levels - 2
        (middle,) = call(
            functools.partial(level_inverse, packed=level > 0), [square], [flags, crit, received_crit], 4.5
        )
        back, crit, *others = call(
            functools.partial(level_merge, halved=level > 0, level=level, final=final),
            [pair, packed] + ([square, square] if final else [pair, half_pair]),
            [flags, middle, rest] + received_rest,
            8 if final else 2,
            [pair] * (level > 0),
        )
        received_crit = swapped(crit, 2 ** (level + 1))
        if not final:
            rest, rest_half = others
            arrived = swapped(rest_half, 2 ** (level + 1))
            received_rest = [arrived, swapped(arrived, 1)]
        else:
            end, far = others
        split = level == 0
        columns = wide if split else narrow
        value, *others = call(
            functools.partial(level_sides, level=level, split=split, final=final),
            [columns] + ([columns, columns] if final else [(2,) + narrow, (2,) + narrow] if split else [(2,) + columns]),
            [flags, middle, back, sides, received_sides] + ([far] if final else []),
            1,
        )
        if final:
            own, ends = others
            received_own = swapped(own, 2 ** (level + 1))
        else:
            sides = others[0]
            received_sides = swapped(others[-1], 2 ** (level + 1))
        backs.append(back)
        values.append(value)
    (root,) = call(functools.partial(level_inverse, packed=True), [square], [flags, crit, received_crit], 4.5)
    keep, send = call(
        functools.partial(descend, levels=levels),
        [(2,) + narrow, (2,) + narrow],
        [flags, root, own, received_own, end, far, ends] + backs[1:] + values[1:],
        2,
    )
    received = swapped(send, 2)
    keep, send = call(
        descend_last, [(2,) + wide, (2,) + wide], [flags, keep, received, backs[0], values[0]], 1
    )
    received = swapped(send, 1)
    (out,) = call(
        functools.partial(finish, width=width, classes=classes),
        [(blocks * width, classes)],
        [flags, keep, received, spikes, interior],
        3,
        [(2 * width, classes), (3, width, classes), pltpu.SemaphoreType.DMA((4,))],
        out_hbm=True,
    )
    return out


def solution(mesh):
    in_specs = (P("slab", None, None), P("slab", None, None), P("slab"), P("slab"))
    out_specs = P("slab", None)
    return jax.shard_map(shards, mesh=mesh, in_specs=in_specs, out_specs=out_specs, check_vma=False)
```

```python
import functools

import jax
import jax.numpy as jnp
from jax import lax
from jax.experimental import pallas as pl
from jax.experimental.pallas import tpu as pltpu
from jax.sharding import PartitionSpec as P

C = 512

alpha_rate = 0.995

f32 = jnp.float32
bf16 = jnp.bfloat16

NN = (((1,), (0,)), ((), ()))
NT = (((1,), (1,)), ((), ()))
TN = (((0,), (0,)), ((), ()))


def product(left, right, dims=NN):
    return lax.dot_general(left, right, dims, precision=lax.Precision.HIGHEST, preferred_element_type=f32)


def single(left, right, dims=NN):
    return lax.dot_general(left, right, dims, preferred_element_type=f32)


def halves(array):
    high = array.astype(bf16)
    return high, (array - high.astype(f32)).astype(bf16)


def product3(left, right, dims=NN):
    left_high, left_low = halves(left)
    right_high, right_low = halves(right)
    return single(left_high, right_high, dims) + (
        single(left_high, right_low, dims) + single(left_low, right_high, dims)
    )


def narrow_product(left, right):
    return single(left.astype(bf16), right.astype(bf16))


def unit(width):
    rows = lax.broadcasted_iota(jnp.int32, (width, width), 0)
    columns = lax.broadcasted_iota(jnp.int32, (width, width), 1)
    return (rows == columns).astype(f32)


DOUBLINGS = 6


def inverses(matrices):
    width = matrices[0].shape[0]
    identity = unit(width)
    scale = 1.0 / alpha_rate
    residuals = [identity - matrix for matrix in matrices]
    results = [identity for _ in matrices]
    for step in range(DOUBLINGS):
        following = 2.0 * scale * scale - 1.0
        gain = 2.0 * scale * scale / following
        next_residuals, next_results = [], []
        for residual, result in zip(residuals, results):
            if step == 0:
                next_residuals.append(gain * product3(residual, residual) - identity * (1.0 / following))
                next_results.append(gain * (identity + residual))
            elif step < DOUBLINGS - 1:
                both = product3(jnp.concatenate([residual, result], axis=0), residual)
                next_residuals.append(gain * both[:width] - identity * (1.0 / following))
                next_results.append(gain * (result + both[width:]))
            else:
                next_residuals.append(residual)
                next_results.append(gain * (result + product3(result, residual)))
        residuals, results = next_residuals, next_results
        scale = following
    errors = [identity - product(matrix, result) for matrix, result in zip(matrices, results)]
    squares = [narrow_product(error, error) for error in errors]
    cubes = [narrow_product(error, square) for error, square in zip(errors, squares)]
    return [
        result + product3(result, error + (square + cube))
        for result, error, square, cube in zip(results, errors, squares, cubes)
    ]


def call(kernel, shapes, operands, microseconds, scratch=(), hbm=(), out_hbm=False, limit=12):
    in_specs = [pl.BlockSpec(memory_space=pltpu.VMEM) for _ in operands]
    in_specs[0] = pl.BlockSpec(memory_space=pltpu.SMEM)
    for index in hbm:
        in_specs[index] = pl.BlockSpec(memory_space=pltpu.HBM)
    return pl.pallas_call(
        kernel,
        out_shape=[jax.ShapeDtypeStruct(shape, f32) for shape in shapes],
        in_specs=in_specs,
        out_specs=[pl.BlockSpec(memory_space=pltpu.HBM if out_hbm else pltpu.VMEM) for _ in shapes],
        scratch_shapes=[pltpu.VMEM(shape, f32) if isinstance(shape, tuple) else shape for shape in scratch],
        cost_estimate=pl.CostEstimate(flops=int(microseconds * 1.1e9), bytes_accessed=0, transcendentals=0),
        compiler_params=pltpu.CompilerParams(vmem_limit_bytes=limit * 2**20),
    )(*operands)


def join_rows(target, mine, other, core):
    half = mine.shape[-2]
    target[..., pl.ds(pl.multiple_of(core * half, half), half), :] = mine[...]
    target[..., pl.ds(pl.multiple_of((1 - core) * half, half), half), :] = other[...]


def pack(matrix, out):
    half = matrix.shape[0] // 2
    rows = lax.broadcasted_iota(jnp.int32, (half, half), 0)
    columns = lax.broadcasted_iota(jnp.int32, (half, half), 1)
    last = matrix[half:, half:]
    out[:half, :half] = matrix[half:, :half]
    out[:half, half:] = jnp.where(rows >= columns, matrix[:half, :half], last)
    diagonal = jnp.sum(jnp.where(rows == columns, last, 0.0), axis=0, keepdims=True)
    out[half:, half:] = jnp.broadcast_to(diagonal, (8, half))
    out[half:, :half] = jnp.zeros((8, half), f32)


def unpack(packed):
    half = packed.shape[1] // 2
    rows = lax.broadcasted_iota(jnp.int32, (half, half), 0)
    columns = lax.broadcasted_iota(jnp.int32, (half, half), 1)
    corner = packed[:half, :half]
    both = packed[:half, half:]
    flipped = both.T
    diagonal = packed[half : half + 1, half:]
    first = jnp.where(rows >= columns, both, flipped)
    last = jnp.where(rows < columns, both, jnp.where(rows > columns, flipped, diagonal))
    return jnp.concatenate(
        [jnp.concatenate([first, corner.T], axis=1), jnp.concatenate([corner, last], axis=1)], axis=0
    )


def local_factor(flags, diag_in, coupling_in, inverse_out, link_out, crit, rest, diag, coupling, sems, *, width):
    copies = []
    for i in (0, 2, 1, 3):
        copies.append(pltpu.make_async_copy(diag_in.at[i], diag.at[i], sems.at[i]))
    for i in range(4):
        copies.append(pltpu.make_async_copy(coupling_in.at[i], coupling.at[i], sems.at[4 + i]))
    for copy in copies:
        copy.start()
    identity = unit(width)
    copies[0].wait()
    copies[1].wait()
    v0, v2 = inverses([identity - alpha_rate * diag[0], identity - alpha_rate * diag[2]])
    for copy in copies[2:]:
        copy.wait()
    d1 = identity - alpha_rate * diag[1]
    d3 = identity - alpha_rate * diag[3]
    l = [-alpha_rate * coupling[i] for i in range(4)]
    l[0] = jnp.where(flags[1] == 1, 0.0, l[0])
    v0_l1t = product(v0, l[1], NT)
    v2_l2 = product(v2, l[2])
    middle = d1 - product(l[1], v0_l1t) - product(l[2], v2_l2, TN)
    (v1,) = inverses([middle])
    v0_l0 = product(v0, l[0])
    v2_l3t = product(v2, l[3], NT)
    g = -product(l[1], v0_l0)
    h = -product(l[2], v2_l3t, TN)
    v1_g = product(v1, g)
    v1_h = product(v1, h)
    left = -product(l[0], v0_l0, TN) - product(g, v1_g, TN)
    right = d3 - product(l[3], v2_l3t) - product(h, v1_h, TN)
    across = -product(g, v1_h, TN)
    crit[...] = jnp.where(flags[2] == 0, right, left)
    rest[0] = jnp.where(flags[2] == 0, left, right)
    rest[1] = across
    inverse_out[0] = v0
    inverse_out[1] = v1
    inverse_out[2] = v2
    for i, value in enumerate((v0_l0, v0_l1t, v1_g, v1_h, v2_l2, v2_l3t)):
        link_out[i] = value


def local_sides(flags, seeds, inverse, link, keep, send, interior, *, width, classes):
    place = lax.broadcasted_iota(jnp.int32, (width, classes), 1).astype(f32)
    turned = seeds[...].T
    b = [jnp.where(turned[:, i : i + 1] == place, turned[:, 4 + i : 5 + i], 0.0) for i in range(4)]
    b1 = b[1] - product3(link[1], b[0], TN) - product3(link[4], b[2], TN)
    left = -product3(link[0], b[0], TN) - product3(link[2], b1, TN)
    right = b[3] - product3(link[5], b[2], TN) - product3(link[3], b1, TN)
    interior[0] = b[0]
    interior[1] = b1
    interior[2] = b[2]
    lower = flags[0] == 0
    half = classes // 2
    crit = jnp.where(lower, right, left)
    rest = jnp.where(lower, left, right)
    keep[0] = jnp.where(lower, crit[:, :half], crit[:, half:])
    keep[1] = jnp.where(lower, rest[:, :half], rest[:, half:])
    send[0] = jnp.where(lower, crit[:, half:], crit[:, :half])
    send[1] = jnp.where(lower, rest[:, half:], rest[:, :half])


def local_spikes(flags, inverse, link, sides, spikes, interior, *, width):
    y1 = product3(inverse[1], sides[1])
    interior[1] = y1
    interior[0] = product3(inverse[0], sides[0]) - product3(link[1], y1)
    interior[2] = product3(inverse[2], sides[2]) - product3(link[4], y1)
    s1 = jnp.concatenate([link[2], link[3]], axis=1)
    spikes[1] = s1
    first = -product3(link[1], s1)
    spikes[0, :, :width] = first[:, :width] + link[0]
    spikes[0, :, width:] = first[:, width:]
    last = -product3(link[4], s1)
    spikes[2, :, :width] = last[:, :width]
    spikes[2, :, width:] = last[:, width:] + link[5]


def level_inverse(flags, crit, received, out, *, packed):
    total = crit[...] + received[...]
    (inverse,) = inverses([unpack(total) if packed else total])
    out[...] = inverse


def level_crit(flags, inverse, rest, received, *refs, halved, level):
    if halved:
        other, crit_out, scaled_out, whole = refs
        join_rows(whole, received, other, flags[0])
        received = whole
    else:
        crit_out, scaled_out = refs
    lower = flags[2 + level] == 0
    next_lower = flags[3 + level] == 0
    from_received = lower == next_lower
    base = jnp.where(from_received, received[0], rest[0])
    link = jnp.where(from_received, received[1], rest[1])
    link = jnp.where(next_lower, link, link.T)
    scaled = product(inverse[...], link)
    scaled_out[...] = scaled
    pack(base - product(link, scaled, TN), crit_out)


def level_rest(flags, inverse, scaled, rest, received, *refs, halved, level):
    if halved:
        other, back, rest_out, rest_half, whole = refs
        join_rows(whole, received, other, flags[0])
        received = whole
    else:
        back, rest_out, rest_half = refs
    lower = flags[2 + level] == 0
    next_lower = flags[3 + level] == 0
    from_received = lower == next_lower
    base = jnp.where(from_received, rest[0], received[0])
    link = jnp.where(from_received, rest[1], received[1])
    near = jnp.where(from_received, received[1], rest[1])
    link = jnp.where(next_lower, link.T, link)
    other = product(inverse[...], link)
    rest_out[0] = base - product(link, other, TN)
    to_left = jnp.where(next_lower, other, scaled[...])
    to_right = jnp.where(next_lower, scaled[...], other)
    back[0] = to_left
    back[1] = to_right
    rest_out[1] = -product(jnp.where(next_lower, link.T, near), to_right)
    half = rest_half.shape[1]
    rest_half[...] = rest_out[:, pl.ds(pl.multiple_of(flags[0] * half, half), half), :]


def level_end(flags, inverse, rest, received, other, back, crit_out, end, far, whole, *, level):
    join_rows(whole, received, other, flags[0])
    received = whole
    lower = flags[2 + level] == 0
    a_left = jnp.where(lower, rest[0], received[0])
    b_left = jnp.where(lower, rest[1], received[1])
    c_right = jnp.where(lower, received[0], rest[0])
    b_right = jnp.where(lower, received[1], rest[1])
    to_left = product(inverse[...], b_left, NT)
    to_right = product(inverse[...], b_right)
    left = a_left - product(b_left, to_left)
    right = c_right - product(b_right, to_right, TN)
    across = -product(b_left, to_right)
    back[0] = to_left
    back[1] = to_right
    (last,) = inverses([right])
    end[...] = last
    scaled = product(across, last)
    far[...] = scaled
    pack(jnp.where(flags[3 + level] == 0, right, left - product(scaled, across, NT)), crit_out)


def level_sides(flags, inverse, back, own, received, *refs, level, split, final):
    lower = flags[2 + level] == 0
    g = own[0] + received[0]
    a_left = jnp.where(lower, own[1], received[1])
    c_right = jnp.where(lower, received[1], own[1])
    left = a_left - product3(back[0], g, TN)
    right = c_right - product3(back[1], g, TN)
    next_lower = flags[3 + level] == 0
    if final:
        far, value, out, ends = refs
        ends[...] = right
        out[...] = jnp.where(next_lower, right, left - product3(far[...], right))
    else:
        crit = jnp.where(next_lower, right, left)
        rest = jnp.where(next_lower, left, right)
        if split:
            value, keep, send = refs
            half = crit.shape[1] // 2
            for i, side in enumerate((crit, rest)):
                keep[i] = jnp.where(next_lower, side[:, :half], side[:, half:])
                send[i] = jnp.where(next_lower, side[:, half:], side[:, :half])
        else:
            value, out = refs
            out[0] = crit
            out[1] = rest
    value[...] = product3(inverse[...], g)


def descend(flags, *refs, levels):
    root, own, received, end, far, ends = refs[:6]
    count = levels - 2
    backs, values = refs[6 : 6 + count], refs[6 + count : 6 + 2 * count]
    keep, send = refs[-2:]
    lower = flags[2 + levels - 1] == 0
    q = product3(root[...], own[...] + received[...])
    outer = product3(end[...], ends[...]) - product3(far[...], q, TN)
    p = jnp.where(lower, 0.0, q)
    r = jnp.where(lower, q, outer)
    for level in range(levels - 2, 0, -1):
        q = values[level - 1][...] - product3(backs[level - 1][0], p) - product3(backs[level - 1][1], r)
        lower = flags[2 + level] == 0
        pair = (jnp.where(lower, p, q), jnp.where(lower, q, r))
        if level > 1:
            p, r = pair
    keep[0], keep[1] = pair
    send[0] = jnp.where(lower, q, p)
    send[1] = jnp.where(lower, r, q)


def descend_last(flags, mine, other, back, value, keep, send):
    lower = flags[3] == 0
    p, r = [
        jnp.concatenate([jnp.where(lower, mine[i], other[i]), jnp.where(lower, other[i], mine[i])], axis=1)
        for i in range(2)
    ]
    q = value[...] - product3(back[0], p) - product3(back[1], r)
    lower = flags[2] == 0
    keep[0] = jnp.where(lower, p, q)
    keep[1] = jnp.where(lower, q, r)
    send[0] = jnp.where(lower, q, p)
    send[1] = jnp.where(lower, r, q)


def finish(flags, keep, received, spikes, interior, out, ends, rows, sems, *, width, classes):
    half = classes // 2
    lower = flags[0] == 0
    for i in range(2):
        ends[i * width : (i + 1) * width, :half] = jnp.where(lower, keep[i], received[i])
        ends[i * width : (i + 1) * width, half:] = jnp.where(lower, received[i], keep[i])
    copies = [pltpu.make_async_copy(ends.at[pl.ds(width, width)], out.at[pl.ds(3 * width, width)], sems.at[3])]
    copies[0].start()
    for i in range(3):
        rows[i] = interior[i] - product3(spikes[i], ends[...])
        copies.append(pltpu.make_async_copy(rows.at[i], out.at[pl.ds(i * width, width)], sems.at[i]))
        copies[-1].start()
    for copy in copies:
        copy.wait()


def swapped(array, distance):
    length = lax.axis_size("slab")
    return lax.ppermute(array, "slab", [(i, i ^ distance) for i in range(length)])


def shards(diag_tiles, coupling, labels, confidence):
    blocks, width, _ = diag_tiles.shape
    classes = C
    square, pair, half_pair = (width, width), (2, width, width), (2, width // 2, width)
    packed = (width // 2 + 8, width)
    wide, narrow = (width, classes // 2), (width, classes // 4)
    levels = lax.axis_size("slab").bit_length() - 1
    position = lax.axis_index("slab")
    flags = jnp.stack([position & 1, (position == 0).astype(jnp.int32)] + [(position >> k) & 1 for k in range(levels)])
    seeds = jnp.concatenate([labels.reshape(blocks, width).astype(f32), confidence.reshape(blocks, width)], axis=0)
    diag_tiles = pltpu.with_memory_space_constraint(diag_tiles, pltpu.HBM)
    coupling = pltpu.with_memory_space_constraint(coupling, pltpu.HBM)
    inverse, link, crit, rest = call(
        functools.partial(local_factor, width=width),
        [(3,) + square, (6,) + square, square, pair],
        [flags, diag_tiles, coupling],
        13,
        [(4,) + square, (4,) + square, pltpu.SemaphoreType.DMA((8,))],
        (1, 2),
    )
    received_crit = swapped(crit, 1)
    received_rest = [swapped(rest, 1)]
    sides, send, inner = call(
        functools.partial(local_sides, width=width, classes=classes),
        [(2,) + wide, (2,) + wide, (3, width, classes)],
        [flags, seeds, inverse, link],
        3,
    )
    received_crit, send = lax.optimization_barrier((received_crit, send))
    received_sides = swapped(send, 1)
    backs, values = [], []
    for level in range(levels - 1):
        final = level == levels - 2
        halved = level > 0
        (middle,) = call(
            functools.partial(level_inverse, packed=halved), [square], [flags, crit, received_crit], 4.5
        )
        if halved:
            arrived, middle = lax.optimization_barrier((received_rest, middle))
            received_rest = [arrived, swapped(arrived, 1)]
            if final:
                send, middle = lax.optimization_barrier((send, middle))
        scratch = [pair] * halved
        if final:
            back, crit, end, far = call(
                functools.partial(level_end, level=level),
                [pair, packed, square, square],
                [flags, middle, rest] + received_rest,
                7,
                scratch,
            )
            received_crit = swapped(crit, 2 ** (level + 1))
            far, inner = lax.optimization_barrier((far, inner))
            spikes, interior = call(
                functools.partial(local_spikes, width=width),
                [(3, width, 2 * width), (3, width, classes)],
                [flags, inverse, link, inner],
                3,
            )
            far, spikes, interior = lax.optimization_barrier((far, spikes, interior))
        else:
            crit, scaled = call(
                functools.partial(level_crit, halved=halved, level=level),
                [packed, square],
                [flags, middle, rest] + received_rest,
                1.2,
                scratch,
            )
            if halved:
                crit, send = lax.optimization_barrier((crit, send))
            received_crit = swapped(crit, 2 ** (level + 1))
            back, rest, rest_half = call(
                functools.partial(level_rest, halved=halved, level=level),
                [pair, pair, half_pair],
                [flags, middle, scaled, rest] + received_rest,
                1.2,
                scratch,
            )
            received_rest = swapped(rest_half, 2 ** (level + 1))
        if halved:
            received_sides = swapped(send, 2**level)
        split = level == 0
        columns = wide if split else narrow
        value, *others = call(
            functools.partial(level_sides, level=level, split=split, final=final),
            [columns] + ([columns, columns] if final else [(2,) + narrow, (2,) + narrow] if split else [(2,) + columns]),
            [flags, middle, back, sides, received_sides] + ([far] if final else []),
            1,
        )
        if final:
            own, ends = others
            received_own = swapped(own, 2 ** (level + 1))
        else:
            sides, send = others[0], others[-1]
        backs.append(back)
        values.append(value)
    (root,) = call(functools.partial(level_inverse, packed=True), [square], [flags, crit, received_crit], 4.5)
    keep, send = call(
        functools.partial(descend, levels=levels),
        [(2,) + narrow, (2,) + narrow],
        [flags, root, own, received_own, end, far, ends] + backs[1:] + values[1:],
        2,
    )
    received = swapped(send, 2)
    keep, send = call(
        descend_last, [(2,) + wide, (2,) + wide], [flags, keep, received, backs[0], values[0]], 1
    )
    received = swapped(send, 1)
    (out,) = call(
        functools.partial(finish, width=width, classes=classes),
        [(blocks * width, classes)],
        [flags, keep, received, spikes, interior],
        3,
        [(2 * width, classes), (3, width, classes), pltpu.SemaphoreType.DMA((4,))],
        out_hbm=True,
    )
    return out


def solution(mesh):
    in_specs = (P("slab", None, None), P("slab", None, None), P("slab"), P("slab"))
    out_specs = P("slab", None)
    return jax.shard_map(shards, mesh=mesh, in_specs=in_specs, out_specs=out_specs, check_vma=False)
```

```python
import functools

import jax
import jax.numpy as jnp
from jax import lax
from jax.experimental import pallas as pl
from jax.experimental.pallas import tpu as pltpu
from jax.sharding import PartitionSpec as P

C = 512

alpha_rate = 0.995

f32 = jnp.float32
bf16 = jnp.bfloat16

NN = (((1,), (0,)), ((), ()))
NT = (((1,), (1,)), ((), ()))
TN = (((0,), (0,)), ((), ()))


def product(left, right, dims=NN):
    return lax.dot_general(left, right, dims, precision=lax.Precision.HIGHEST, preferred_element_type=f32)


def single(left, right, dims=NN):
    return lax.dot_general(left, right, dims, preferred_element_type=f32)


def halves(array):
    high = array.astype(bf16)
    return high, (array - high.astype(f32)).astype(bf16)


def product3(left, right, dims=NN):
    left_high, left_low = halves(left)
    right_high, right_low = halves(right)
    return single(left_high, right_high, dims) + (
        single(left_high, right_low, dims) + single(left_low, right_high, dims)
    )


def narrow_product(left, right):
    return single(left.astype(bf16), right.astype(bf16))


def unit(width):
    rows = lax.broadcasted_iota(jnp.int32, (width, width), 0)
    columns = lax.broadcasted_iota(jnp.int32, (width, width), 1)
    return (rows == columns).astype(f32)


DOUBLINGS = 6


def inverses(matrices):
    width = matrices[0].shape[0]
    identity = unit(width)
    scale = 1.0 / alpha_rate
    residuals = [identity - matrix for matrix in matrices]
    results = [identity for _ in matrices]
    for step in range(DOUBLINGS):
        following = 2.0 * scale * scale - 1.0
        gain = 2.0 * scale * scale / following
        next_residuals, next_results = [], []
        for residual, result in zip(residuals, results):
            if step == 0:
                next_residuals.append(gain * product3(residual, residual) - identity * (1.0 / following))
                next_results.append(gain * (identity + residual))
            elif step < DOUBLINGS - 1:
                both = product3(jnp.concatenate([residual, result], axis=0), residual)
                next_residuals.append(gain * both[:width] - identity * (1.0 / following))
                next_results.append(gain * (result + both[width:]))
            else:
                next_residuals.append(residual)
                next_results.append(gain * (result + product3(result, residual)))
        residuals, results = next_residuals, next_results
        scale = following
    errors = [identity - product(matrix, result) for matrix, result in zip(matrices, results)]
    squares = [narrow_product(error, error) for error in errors]
    cubes = [narrow_product(error, square) for error, square in zip(errors, squares)]
    return [
        result + product3(result, error + (square + cube))
        for result, error, square, cube in zip(results, errors, squares, cubes)
    ]


def call(kernel, shapes, operands, microseconds, scratch=(), hbm=(), out_hbm=(), alias={}):
    in_specs = [pl.BlockSpec(memory_space=pltpu.VMEM) for _ in operands]
    in_specs[0] = pl.BlockSpec(memory_space=pltpu.SMEM)
    for index in hbm:
        in_specs[index] = pl.BlockSpec(memory_space=pltpu.HBM)
    return pl.pallas_call(
        kernel,
        out_shape=[pltpu.HBM(s, f32) if i in out_hbm else jax.ShapeDtypeStruct(s, f32) for i, s in enumerate(shapes)],
        in_specs=in_specs,
        out_specs=[pl.BlockSpec(memory_space=pltpu.HBM if i in out_hbm else pltpu.VMEM) for i in range(len(shapes))],
        input_output_aliases=alias,
        scratch_shapes=[pltpu.VMEM(shape, f32) if isinstance(shape, tuple) else shape for shape in scratch],
        cost_estimate=pl.CostEstimate(flops=int(microseconds * 1.1e9), bytes_accessed=0, transcendentals=0),
        compiler_params=pltpu.CompilerParams(vmem_limit_bytes=12 * 2**20),
    )(*operands)


def join_rows(target, mine, other, core):
    half = mine.shape[-2]
    target[..., pl.ds(pl.multiple_of(core * half, half), half), :] = mine[...]
    target[..., pl.ds(pl.multiple_of((1 - core) * half, half), half), :] = other[...]


def pack(matrix, out):
    half = matrix.shape[0] // 2
    rows = lax.broadcasted_iota(jnp.int32, (half, half), 0)
    columns = lax.broadcasted_iota(jnp.int32, (half, half), 1)
    last = matrix[half:, half:]
    out[:half, :half] = matrix[half:, :half]
    out[:half, half:] = jnp.where(rows >= columns, matrix[:half, :half], last)
    diagonal = jnp.sum(jnp.where(rows == columns, last, 0.0), axis=0, keepdims=True)
    out[half:, half:] = jnp.broadcast_to(diagonal, (8, half))
    out[half:, :half] = jnp.zeros((8, half), f32)


def unpack(packed):
    half = packed.shape[1] // 2
    rows = lax.broadcasted_iota(jnp.int32, (half, half), 0)
    columns = lax.broadcasted_iota(jnp.int32, (half, half), 1)
    corner = packed[:half, :half]
    both = packed[:half, half:]
    flipped = both.T
    diagonal = packed[half : half + 1, half:]
    first = jnp.where(rows >= columns, both, flipped)
    last = jnp.where(rows < columns, both, jnp.where(rows > columns, flipped, diagonal))
    return jnp.concatenate(
        [jnp.concatenate([first, corner.T], axis=1), jnp.concatenate([corner, last], axis=1)], axis=0
    )


def local_factor(flags, diag_in, coupling_in, inverse_out, link_out, crit, rest, diag, coupling, inner, sems, *, width):
    copies = []
    for i in (0, 2, 1, 3):
        copies.append(pltpu.make_async_copy(diag_in.at[i], diag.at[i], sems.at[i]))
    for i in range(4):
        copies.append(pltpu.make_async_copy(coupling_in.at[i], coupling.at[i], sems.at[4 + i]))
    for copy in copies:
        copy.start()
    identity = unit(width)
    copies[0].wait()
    copies[1].wait()
    v0, v2 = inverses([identity - alpha_rate * diag[0], identity - alpha_rate * diag[2]])
    for copy in copies[2:]:
        copy.wait()
    inner[0] = v0
    inner[2] = v2
    copies = [pltpu.make_async_copy(inner.at[i], inverse_out.at[i], sems.at[8 + i]) for i in range(3)]
    copies[0].start()
    copies[2].start()
    d1 = identity - alpha_rate * diag[1]
    d3 = identity - alpha_rate * diag[3]
    l = [-alpha_rate * coupling[i] for i in range(4)]
    l[0] = jnp.where(flags[1] == 1, 0.0, l[0])
    v0_l1t = product3(v0, l[1], NT)
    v2_l2 = product3(v2, l[2])
    middle = d1 - product3(l[1], v0_l1t) - product3(l[2], v2_l2, TN)
    (v1,) = inverses([middle])
    inner[1] = v1
    copies[1].start()
    v0_l0 = product3(v0, l[0])
    v2_l3t = product3(v2, l[3], NT)
    g = -product3(l[1], v0_l0)
    h = -product3(l[2], v2_l3t, TN)
    v1_g = product3(v1, g)
    v1_h = product3(v1, h)
    left = -product3(l[0], v0_l0, TN) - product3(g, v1_g, TN)
    right = d3 - product3(l[3], v2_l3t) - product3(h, v1_h, TN)
    across = -product3(g, v1_h, TN)
    crit[...] = jnp.where(flags[2] == 0, right, left)
    rest[0] = jnp.where(flags[2] == 0, left, right)
    rest[1] = across
    for i, value in enumerate((v0_l0, v0_l1t, v1_g, v1_h, v2_l2, v2_l3t)):
        link_out[i] = value
    for copy in copies:
        copy.wait()


def local_sides(flags, seeds, link, keep, send, interior, *, width, classes):
    place = lax.broadcasted_iota(jnp.int32, (width, classes), 1).astype(f32)
    turned = seeds[...].T
    b = [jnp.where(turned[:, i : i + 1] == place, turned[:, 4 + i : 5 + i], 0.0) for i in range(4)]
    b1 = b[1] - product3(link[1], b[0], TN) - product3(link[4], b[2], TN)
    left = -product3(link[0], b[0], TN) - product3(link[2], b1, TN)
    right = b[3] - product3(link[5], b[2], TN) - product3(link[3], b1, TN)
    interior[0] = b[0]
    interior[1] = b1
    interior[2] = b[2]
    lower = flags[0] == 0
    half = classes // 2
    crit = jnp.where(lower, right, left)
    rest = jnp.where(lower, left, right)
    keep[0] = jnp.where(lower, crit[:, :half], crit[:, half:])
    keep[1] = jnp.where(lower, rest[:, :half], rest[:, half:])
    send[0] = jnp.where(lower, crit[:, half:], crit[:, :half])
    send[1] = jnp.where(lower, rest[:, half:], rest[:, :half])


def local_spikes(flags, inverse_in, link, sides, spikes, interior, inverse, sem, *, width):
    copy = pltpu.make_async_copy(inverse_in, inverse, sem)
    copy.start()
    s1 = jnp.concatenate([link[2], link[3]], axis=1)
    spikes[1] = s1
    first = -product3(link[1], s1)
    spikes[0, :, :width] = first[:, :width] + link[0]
    spikes[0, :, width:] = first[:, width:]
    last = -product3(link[4], s1)
    spikes[2, :, :width] = last[:, :width]
    spikes[2, :, width:] = last[:, width:] + link[5]
    copy.wait()
    y1 = product3(inverse[1], sides[1])
    interior[1] = y1
    interior[0] = product3(inverse[0], sides[0]) - product3(link[1], y1)
    interior[2] = product3(inverse[2], sides[2]) - product3(link[4], y1)


def level_inverse(flags, crit, received, out, *, packed):
    total = crit[...] + received[...]
    (inverse,) = inverses([unpack(total) if packed else total])
    out[...] = inverse


def gather_packed(packed, mine, other, core):
    rows = mine.shape[0] - 8
    packed[pl.ds(pl.multiple_of(core * rows, 8), rows + 8), :] = mine[...]
    packed[pl.ds(pl.multiple_of((1 - core) * rows, 8), rows + 8), :] = other[...]


def gather_rest(whole, mine, other, core):
    half = whole.shape[1] // 2
    join_rows(whole.at[1], mine.at[:half], other.at[:half], core)
    gather_packed(whole.at[0], mine.at[half:], other.at[half:], core)
    whole[0] = unpack(whole[0, : half + 8, :])


def level_crit(flags, inverse, rest, received, *refs, halved, level):
    if halved:
        other, crit_out, scaled_out, whole = refs
        gather_rest(whole, received, other, flags[0])
        received = whole
    else:
        crit_out, scaled_out = refs
    lower = flags[2 + level] == 0
    next_lower = flags[3 + level] == 0
    from_received = lower == next_lower
    base = jnp.where(from_received, received[0], rest[0])
    link = jnp.where(from_received, received[1], rest[1])
    link = jnp.where(next_lower, link, link.T)
    scaled = product3(inverse[...], link)
    scaled_out[...] = scaled
    pack(base - product3(link, scaled, TN), crit_out)


def level_rest(flags, inverse, scaled, rest, received, back, rest_out, message, packed, *, level):
    lower = flags[2 + level] == 0
    next_lower = flags[3 + level] == 0
    from_received = lower == next_lower
    base = jnp.where(from_received, rest[0], received[0])
    link = jnp.where(from_received, rest[1], received[1])
    near = jnp.where(from_received, received[1], rest[1])
    link = jnp.where(next_lower, link.T, link)
    other = product3(inverse[...], link)
    matrix = base - product3(link, other, TN)
    rest_out[0] = matrix
    to_left = jnp.where(next_lower, other, scaled[...])
    to_right = jnp.where(next_lower, scaled[...], other)
    back[0] = to_left
    back[1] = to_right
    rest_out[1] = -product3(jnp.where(next_lower, link.T, near), to_right)
    half = matrix.shape[0] // 2
    message[:half, :] = rest_out[1, pl.ds(pl.multiple_of(flags[0] * half, half), half), :]
    pack(matrix, packed)
    rows = half // 2
    message[half:, :] = packed[pl.ds(pl.multiple_of(flags[0] * rows, 8), rows + 8), :]


def level_end(flags, inverse, rest, received, other, back, crit_out, end, far, message, whole, *, level):
    gather_rest(whole, received, other, flags[0])
    received = whole
    lower = flags[2 + level] == 0
    a_left = jnp.where(lower, rest[0], received[0])
    b_left = jnp.where(lower, rest[1], received[1])
    c_right = jnp.where(lower, received[0], rest[0])
    b_right = jnp.where(lower, received[1], rest[1])
    to_left = product3(inverse[...], b_left, NT)
    to_right = product3(inverse[...], b_right)
    left = a_left - product3(b_left, to_left)
    right = c_right - product3(b_right, to_right, TN)
    across = -product3(b_left, to_right)
    back[0] = to_left
    back[1] = to_right
    (last,) = inverses([right])
    end[...] = last
    scaled = product3(across, last)
    far[...] = scaled
    pack(jnp.where(flags[3 + level] == 0, right, left - product3(scaled, across, NT)), crit_out)
    rows = message.shape[0] - 8
    message[...] = crit_out[pl.ds(pl.multiple_of(flags[0] * rows, 8), rows + 8), :]


def level_sides(flags, inverse, back, own, received, *refs, level, split, final):
    lower = flags[2 + level] == 0
    g = own[0] + received[0]
    a_left = jnp.where(lower, own[1], received[1])
    c_right = jnp.where(lower, received[1], own[1])
    left = a_left - product3(back[0], g, TN)
    right = c_right - product3(back[1], g, TN)
    next_lower = flags[3 + level] == 0
    if final:
        far, end, value, out, outer = refs
        out[...] = jnp.where(next_lower, right, left - product3(far[...], right))
    else:
        crit = jnp.where(next_lower, right, left)
        rest = jnp.where(next_lower, left, right)
        if split:
            value, keep, send = refs
            half = crit.shape[1] // 2
            for i, side in enumerate((crit, rest)):
                keep[i] = jnp.where(next_lower, side[:, :half], side[:, half:])
                send[i] = jnp.where(next_lower, side[:, half:], side[:, :half])
        else:
            value, out = refs
            out[0] = crit
            out[1] = rest
    value[...] = product3(inverse[...], g)
    if final:
        outer[...] = product3(end[...], right)


def root_inverse(flags, crit, mine, other, out, packed):
    gather_packed(packed, mine, other, flags[0])
    (inverse,) = inverses([unpack(crit[...] + packed[...])])
    out[...] = inverse


def descend(flags, *refs, levels):
    root, own, received, far, outer = refs[:5]
    count = levels - 2
    backs, values = refs[5 : 5 + count], refs[5 + count : 5 + 2 * count]
    keep, send = refs[-2:]
    lower = flags[2 + levels - 1] == 0
    q = product3(root[...], own[...] + received[...])
    outer = outer[...] - product3(far[...], q, TN)
    p = jnp.where(lower, 0.0, q)
    r = jnp.where(lower, q, outer)
    for level in range(levels - 2, 0, -1):
        q = values[level - 1][...] - product3(backs[level - 1][0], p) - product3(backs[level - 1][1], r)
        lower = flags[2 + level] == 0
        pair = (jnp.where(lower, p, q), jnp.where(lower, q, r))
        if level > 1:
            p, r = pair
    keep[0], keep[1] = pair
    send[0] = jnp.where(lower, q, p)
    send[1] = jnp.where(lower, r, q)


def descend_last(flags, mine, back, value, keep, send, *, own):
    half = keep.shape[2]
    place = flags[3] if own else 1 - flags[3]
    p, r = mine[0], mine[1]
    q = value[:, pl.ds(pl.multiple_of(place * half, half), half)] - product3(back[0], p) - product3(back[1], r)
    lower = flags[2] == 0
    keep[0] = jnp.where(lower, p, q)
    keep[1] = jnp.where(lower, q, r)
    send[0] = jnp.where(lower, q, p)
    send[1] = jnp.where(lower, r, q)


def finish(flags, keep, received, spikes, interior, *refs, width, classes, own):
    out, ends, rows, sems = refs[-4:]
    quarter = classes // 4
    place = flags[3] if own else 1 - flags[3]
    columns = [pl.ds(pl.multiple_of(k * 2 * quarter + place * quarter, quarter), quarter) for k in range(2)]
    lower = flags[0] == 0
    copies = []

    def leave(source, block):
        for k in range(2):
            copies.append(
                pltpu.make_async_copy(
                    source.at[:, pl.ds(k * quarter, quarter)],
                    out.at[pl.ds(block * width, width), columns[k]],
                    sems.at[2 * block + k],
                )
            )
            copies[-1].start()

    for i in range(2):
        ends[i * width : (i + 1) * width, :quarter] = jnp.where(lower, keep[i], received[i])
        ends[i * width : (i + 1) * width, quarter:] = jnp.where(lower, received[i], keep[i])
    leave(ends.at[pl.ds(width, width)], 3)
    for i in range(3):
        side = jnp.concatenate([interior[i, :, columns[0]], interior[i, :, columns[1]]], axis=1)
        rows[i] = side - product3(spikes[i], ends[...])
        leave(rows.at[i], i)
    for copy in copies:
        copy.wait()


def swapped(array, distance):
    length = lax.axis_size("slab")
    return lax.ppermute(array, "slab", [(i, i ^ distance) for i in range(length)])


def shards(diag_tiles, coupling, labels, confidence):
    blocks, width, _ = diag_tiles.shape
    classes = C
    square, pair = (width, width), (2, width, width)
    packed, message = (width // 2 + 8, width), (width // 2 + width // 4 + 8, width)
    wide, narrow = (width, classes // 2), (width, classes // 4)
    levels = lax.axis_size("slab").bit_length() - 1
    position = lax.axis_index("slab")
    flags = jnp.stack([position & 1, (position == 0).astype(jnp.int32)] + [(position >> k) & 1 for k in range(levels)])
    seeds = jnp.concatenate([labels.reshape(blocks, width).astype(f32), confidence.reshape(blocks, width)], axis=0)
    diag_tiles = pltpu.with_memory_space_constraint(diag_tiles, pltpu.HBM)
    coupling = pltpu.with_memory_space_constraint(coupling, pltpu.HBM)
    inverse, link, crit, rest = call(
        functools.partial(local_factor, width=width),
        [(3,) + square, (6,) + square, square, pair],
        [flags, diag_tiles, coupling],
        13,
        [(4,) + square, (4,) + square, (3,) + square, pltpu.SemaphoreType.DMA((11,))],
        (1, 2),
        (0,),
    )
    received_crit = swapped(crit, 1)
    received_rest = [swapped(rest, 1)]
    sides, send, inner = call(
        functools.partial(local_sides, width=width, classes=classes),
        [(2,) + wide, (2,) + wide, (3, width, classes)],
        [flags, seeds, link],
        3,
    )
    received_crit, send = lax.optimization_barrier((received_crit, send))
    received_sides = swapped(send, 1)
    backs, values = [], []
    for level in range(levels - 1):
        final = level == levels - 2
        halved = level > 0
        (middle,) = call(
            functools.partial(level_inverse, packed=halved), [square], [flags, crit, received_crit], 4.5
        )
        if halved:
            arrived, middle = lax.optimization_barrier((received_rest, middle))
            received_rest = [arrived, swapped(arrived, 1)]
            if final:
                send, middle = lax.optimization_barrier((send, middle))
        if final:
            back, crit, end, far, message = call(
                functools.partial(level_end, level=level),
                [pair, packed, square, square, (width // 4 + 8, width)],
                [flags, middle, rest] + received_rest,
                7,
                [pair],
            )
            received_crit = swapped(message, 2 ** (level + 1))
        else:
            crit, scaled, *joined = call(
                functools.partial(level_crit, halved=halved, level=level),
                [packed, square] + [pair] * halved,
                [flags, middle, rest] + received_rest,
                1.2,
            )
            if halved:
                crit, send = lax.optimization_barrier((crit, send))
            received_crit = swapped(crit, 2 ** (level + 1))
            back, rest, rest_half = call(
                functools.partial(level_rest, level=level),
                [pair, pair, message],
                [flags, middle, scaled, rest] + (joined or received_rest),
                1.2,
                [packed],
            )
            received_rest = swapped(rest_half, 2 ** (level + 1))
        if halved:
            received_sides = swapped(send, 2**level)
        split = level == 0
        columns = wide if split else narrow
        value, *others = call(
            functools.partial(level_sides, level=level, split=split, final=final),
            [columns] + ([columns, columns] if final else [(2,) + narrow, (2,) + narrow] if split else [(2,) + columns]),
            [flags, middle, back, sides, received_sides] + ([far, end] if final else []),
            0.05 if final else 1,
        )
        if final:
            own, outer = others
            own, inner = lax.optimization_barrier((own, inner))
            spikes, interior = call(
                functools.partial(local_spikes, width=width),
                [(3, width, 2 * width), (3, width, classes)],
                [flags, inverse, link, inner],
                0.05,
                [(3,) + square, pltpu.SemaphoreType.DMA(())],
                (1,),
            )
            received_crit, spikes, interior = lax.optimization_barrier((received_crit, spikes, interior))
            received_own = swapped(own, 2 ** (level + 1))
        else:
            sides, send = others[0], others[-1]
        backs.append(back)
        values.append(value)
    (root,) = call(root_inverse, [square], [flags, crit, received_crit, swapped(received_crit, 1)], 0.05, [packed])
    keep, send = call(
        functools.partial(descend, levels=levels),
        [(2,) + narrow, (2,) + narrow],
        [flags, root, own, received_own, far, outer] + backs[1:] + values[1:],
        2,
    )
    arrived = swapped(send, 2)
    out = []
    for own in (True, False):
        keep, send = call(
            functools.partial(descend_last, own=own),
            [(2,) + narrow, (2,) + narrow],
            [flags, keep if own else arrived, backs[0], values[0]],
            0.7,
        )
        out = call(
            functools.partial(finish, width=width, classes=classes, own=own),
            [(blocks * width, classes)],
            [flags, keep, swapped(send, 1), spikes, interior, *out],
            2,
            [(2 * width, classes // 2), (3, width, classes // 2), pltpu.SemaphoreType.DMA((8,))],
            () if own else (5,),
            (0,),
            {} if own else {5: 0},
        )
    (out,) = out
    return out


def solution(mesh):
    in_specs = (P("slab", None, None), P("slab", None, None), P("slab"), P("slab"))
    out_specs = P("slab", None)
    return jax.shard_map(shards, mesh=mesh, in_specs=in_specs, out_specs=out_specs, check_vma=False)
```

```python
import functools

import jax
import jax.numpy as jnp
from jax import lax
from jax.experimental import pallas as pl
from jax.experimental.pallas import tpu as pltpu
from jax.sharding import PartitionSpec as P

C = 512

alpha_rate = 0.995

f32 = jnp.float32
bf16 = jnp.bfloat16

NN = (((1,), (0,)), ((), ()))
NT = (((1,), (1,)), ((), ()))
TN = (((0,), (0,)), ((), ()))


def product(left, right, dims=NN):
    return lax.dot_general(left, right, dims, precision=lax.Precision.HIGHEST, preferred_element_type=f32)


def single(left, right, dims=NN):
    return lax.dot_general(left, right, dims, preferred_element_type=f32)


def halves(array):
    high = array.astype(bf16)
    return high, (array - high.astype(f32)).astype(bf16)


def product3(left, right, dims=NN):
    left_high, left_low = halves(left)
    right_high, right_low = halves(right)
    return single(left_high, right_high, dims) + (
        single(left_high, right_low, dims) + single(left_low, right_high, dims)
    )


def narrow_product(left, right):
    return single(left.astype(bf16), right.astype(bf16))


def unit(width):
    rows = lax.broadcasted_iota(jnp.int32, (width, width), 0)
    columns = lax.broadcasted_iota(jnp.int32, (width, width), 1)
    return (rows == columns).astype(f32)


DOUBLINGS = 6


def inverses(matrices):
    width = matrices[0].shape[0]
    identity = unit(width)
    scale = 1.0 / alpha_rate
    residuals = [identity - matrix for matrix in matrices]
    results = [identity for _ in matrices]
    for step in range(DOUBLINGS):
        following = 2.0 * scale * scale - 1.0
        gain = 2.0 * scale * scale / following
        for i, (residual, result) in enumerate(zip(residuals, results)):
            high, low = halves(residual)
            both = jnp.concatenate([high, low], axis=1)

            def times(left_high, left_low):
                wide = single(left_high, both)
                return wide[:, :width] + (wide[:, width:] + single(left_low, high))

            if step < DOUBLINGS - 1:
                residuals[i] = gain * times(high, low) - identity * (1.0 / following)
            results[i] = gain * (result + (times(*halves(result)) if step else residual))
        scale = following
    errors = [identity - product(matrix, result) for matrix, result in zip(matrices, results)]
    squares = [narrow_product(error, error) for error in errors]
    cubes = [narrow_product(error, square) for error, square in zip(errors, squares)]
    return [
        result + product3(result, error + (square + cube))
        for result, error, square, cube in zip(results, errors, squares, cubes)
    ]


def call(kernel, shapes, operands, microseconds, scratch=(), hbm=(), out_hbm=(), alias={}):
    in_specs = [pl.BlockSpec(memory_space=pltpu.VMEM) for _ in operands]
    in_specs[0] = pl.BlockSpec(memory_space=pltpu.SMEM)
    for index in hbm:
        in_specs[index] = pl.BlockSpec(memory_space=pltpu.HBM)
    return pl.pallas_call(
        kernel,
        out_shape=[pltpu.HBM(s, f32) if i in out_hbm else jax.ShapeDtypeStruct(s, f32) for i, s in enumerate(shapes)],
        in_specs=in_specs,
        out_specs=[pl.BlockSpec(memory_space=pltpu.HBM if i in out_hbm else pltpu.VMEM) for i in range(len(shapes))],
        input_output_aliases=alias,
        scratch_shapes=[pltpu.VMEM(shape, f32) if isinstance(shape, tuple) else shape for shape in scratch],
        cost_estimate=pl.CostEstimate(flops=int(microseconds * 1.1e9), bytes_accessed=0, transcendentals=0),
        compiler_params=pltpu.CompilerParams(vmem_limit_bytes=12 * 2**20),
    )(*operands)


def join_rows(target, mine, other, core):
    half = mine.shape[-2]
    target[..., pl.ds(pl.multiple_of(core * half, half), half), :] = mine[...]
    target[..., pl.ds(pl.multiple_of((1 - core) * half, half), half), :] = other[...]


def pack(matrix, out):
    half = matrix.shape[0] // 2
    rows = lax.broadcasted_iota(jnp.int32, (half, half), 0)
    columns = lax.broadcasted_iota(jnp.int32, (half, half), 1)
    last = matrix[half:, half:]
    out[:half, :half] = matrix[half:, :half]
    out[:half, half:] = jnp.where(rows >= columns, matrix[:half, :half], last)
    diagonal = jnp.sum(jnp.where(rows == columns, last, 0.0), axis=0, keepdims=True)
    out[half:, half:] = jnp.broadcast_to(diagonal, (8, half))
    out[half:, :half] = jnp.zeros((8, half), f32)


def unpack(packed):
    half = packed.shape[1] // 2
    rows = lax.broadcasted_iota(jnp.int32, (half, half), 0)
    columns = lax.broadcasted_iota(jnp.int32, (half, half), 1)
    corner = packed[:half, :half]
    both = packed[:half, half:]
    flipped = both.T
    diagonal = packed[half : half + 1, half:]
    first = jnp.where(rows >= columns, both, flipped)
    last = jnp.where(rows < columns, both, jnp.where(rows > columns, flipped, diagonal))
    return jnp.concatenate(
        [jnp.concatenate([first, corner.T], axis=1), jnp.concatenate([corner, last], axis=1)], axis=0
    )


def local_factor(flags, diag_in, coupling_in, inverse_out, link_out, crit, rest, diag, coupling, inner, sems, *, width):
    copies = []
    for i in (0, 2, 1, 3):
        copies.append(pltpu.make_async_copy(diag_in.at[i], diag.at[i], sems.at[i]))
    for i in range(4):
        copies.append(pltpu.make_async_copy(coupling_in.at[i], coupling.at[i], sems.at[4 + i]))
    for copy in copies:
        copy.start()
    identity = unit(width)
    copies[0].wait()
    copies[1].wait()
    v0, v2 = inverses([identity - alpha_rate * diag[0], identity - alpha_rate * diag[2]])
    for copy in copies[2:]:
        copy.wait()
    inner[0] = v0
    inner[2] = v2
    copies = [pltpu.make_async_copy(inner.at[i], inverse_out.at[i], sems.at[8 + i]) for i in range(3)]
    copies[0].start()
    copies[2].start()
    d1 = identity - alpha_rate * diag[1]
    d3 = identity - alpha_rate * diag[3]
    l = [-alpha_rate * coupling[i] for i in range(4)]
    l[0] = jnp.where(flags[1] == 1, 0.0, l[0])
    v0_l1t = product3(v0, l[1], NT)
    v2_l2 = product3(v2, l[2])
    middle = d1 - product3(l[1], v0_l1t) - product3(l[2], v2_l2, TN)
    (v1,) = inverses([middle])
    inner[1] = v1
    copies[1].start()
    v0_l0 = product3(v0, l[0])
    v2_l3t = product3(v2, l[3], NT)
    g = -product3(l[1], v0_l0)
    h = -product3(l[2], v2_l3t, TN)
    v1_g = product3(v1, g)
    v1_h = product3(v1, h)
    left = -product3(l[0], v0_l0, TN) - product3(g, v1_g, TN)
    right = d3 - product3(l[3], v2_l3t) - product3(h, v1_h, TN)
    across = -product3(g, v1_h, TN)
    crit[...] = jnp.where(flags[2] == 0, right, left)
    rest[0] = jnp.where(flags[2] == 0, left, right)
    rest[1] = across
    for i, value in enumerate((v0_l0, v0_l1t, v1_g, v1_h, v2_l2, v2_l3t)):
        link_out[i] = value
    for copy in copies:
        copy.wait()


def local_sides(flags, seeds, link, keep, send, interior, *, width, classes):
    place = lax.broadcasted_iota(jnp.int32, (width, classes), 1).astype(f32)
    turned = seeds[...].T
    b = [jnp.where(turned[:, i : i + 1] == place, turned[:, 4 + i : 5 + i], 0.0) for i in range(4)]

    def from_seeds(index, i):
        chosen = jnp.where(turned[:, i : i + 1] == place, 1.0, 0.0).astype(bf16)
        high, low = halves(link[index] * turned[:, 4 + i : 5 + i])
        return single(high, chosen, TN) + single(low, chosen, TN)

    b1 = b[1] - from_seeds(1, 0) - from_seeds(4, 2)
    left = -from_seeds(0, 0) - product3(link[2], b1, TN)
    right = b[3] - from_seeds(5, 2) - product3(link[3], b1, TN)
    interior[0] = b[0]
    interior[1] = b1
    interior[2] = b[2]
    lower = flags[0] == 0
    half = classes // 2
    crit = jnp.where(lower, right, left)
    rest = jnp.where(lower, left, right)
    keep[0] = jnp.where(lower, crit[:, :half], crit[:, half:])
    keep[1] = jnp.where(lower, rest[:, :half], rest[:, half:])
    send[0] = jnp.where(lower, crit[:, half:], crit[:, :half])
    send[1] = jnp.where(lower, rest[:, half:], rest[:, :half])


def local_spikes(flags, inverse_in, link, sides, spikes, interior, inverse, sem, *, width):
    copy = pltpu.make_async_copy(inverse_in, inverse, sem)
    copy.start()
    s1 = jnp.concatenate([link[2], link[3]], axis=1)
    spikes[1] = s1
    first = -product3(link[1], s1)
    spikes[0, :, :width] = first[:, :width] + link[0]
    spikes[0, :, width:] = first[:, width:]
    last = -product3(link[4], s1)
    spikes[2, :, :width] = last[:, :width]
    spikes[2, :, width:] = last[:, width:] + link[5]
    copy.wait()
    y1 = product3(inverse[1], sides[1])
    interior[1] = y1
    interior[0] = product3(inverse[0], sides[0]) - product3(link[1], y1)
    interior[2] = product3(inverse[2], sides[2]) - product3(link[4], y1)


def level_inverse(flags, crit, received, out, *, packed):
    total = crit[...] + received[...]
    (inverse,) = inverses([unpack(total) if packed else total])
    out[...] = inverse


def gather_packed(packed, mine, other, core):
    rows = mine.shape[0] - 8
    packed[pl.ds(pl.multiple_of(core * rows, 8), rows + 8), :] = mine[...]
    packed[pl.ds(pl.multiple_of((1 - core) * rows, 8), rows + 8), :] = other[...]


def gather_rest(whole, mine, other, core):
    half = whole.shape[1] // 2
    join_rows(whole.at[1], mine.at[:half], other.at[:half], core)
    gather_packed(whole.at[0], mine.at[half:], other.at[half:], core)
    whole[0] = unpack(whole[0, : half + 8, :])


def level_crit(flags, inverse, rest, received, *refs, halved, level):
    if halved:
        other, crit_out, scaled_out, whole = refs
        gather_rest(whole, received, other, flags[0])
        received = whole
    else:
        crit_out, scaled_out = refs
    lower = flags[2 + level] == 0
    next_lower = flags[3 + level] == 0
    from_received = lower == next_lower
    base = jnp.where(from_received, received[0], rest[0])
    link = jnp.where(from_received, received[1], rest[1])
    link = jnp.where(next_lower, link, link.T)
    scaled = product3(inverse[...], link)
    scaled_out[...] = scaled
    pack(base - product3(link, scaled, TN), crit_out)


def level_rest(flags, inverse, scaled, rest, received, back, rest_out, message, packed, *, level):
    lower = flags[2 + level] == 0
    next_lower = flags[3 + level] == 0
    from_received = lower == next_lower
    base = jnp.where(from_received, rest[0], received[0])
    link = jnp.where(from_received, rest[1], received[1])
    near = jnp.where(from_received, received[1], rest[1])
    link = jnp.where(next_lower, link.T, link)
    other = product3(inverse[...], link)
    matrix = base - product3(link, other, TN)
    rest_out[0] = matrix
    to_left = jnp.where(next_lower, other, scaled[...])
    to_right = jnp.where(next_lower, scaled[...], other)
    back[0] = to_left
    back[1] = to_right
    rest_out[1] = -product3(jnp.where(next_lower, link.T, near), to_right)
    half = matrix.shape[0] // 2
    message[:half, :] = rest_out[1, pl.ds(pl.multiple_of(flags[0] * half, half), half), :]
    pack(matrix, packed)
    rows = half // 2
    message[half:, :] = packed[pl.ds(pl.multiple_of(flags[0] * rows, 8), rows + 8), :]


def level_end(flags, inverse, rest, received, other, back, crit_out, end, far, message, whole, *, level):
    gather_rest(whole, received, other, flags[0])
    received = whole
    lower = flags[2 + level] == 0
    a_left = jnp.where(lower, rest[0], received[0])
    b_left = jnp.where(lower, rest[1], received[1])
    c_right = jnp.where(lower, received[0], rest[0])
    b_right = jnp.where(lower, received[1], rest[1])
    to_left = product3(inverse[...], b_left, NT)
    to_right = product3(inverse[...], b_right)
    left = a_left - product3(b_left, to_left)
    right = c_right - product3(b_right, to_right, TN)
    across = -product3(b_left, to_right)
    back[0] = to_left
    back[1] = to_right
    (last,) = inverses([right])
    end[...] = last
    scaled = product3(across, last)
    far[...] = scaled
    pack(jnp.where(flags[3 + level] == 0, right, left - product3(scaled, across, NT)), crit_out)
    rows = message.shape[0] - 8
    message[...] = crit_out[pl.ds(pl.multiple_of(flags[0] * rows, 8), rows + 8), :]


def level_sides(flags, inverse, back, own, received, *refs, level, split, final):
    lower = flags[2 + level] == 0
    g = own[0] + received[0]
    a_left = jnp.where(lower, own[1], received[1])
    c_right = jnp.where(lower, received[1], own[1])
    left = a_left - product3(back[0], g, TN)
    right = c_right - product3(back[1], g, TN)
    next_lower = flags[3 + level] == 0
    if final:
        far, end, value, out, outer = refs
        out[...] = jnp.where(next_lower, right, left - product3(far[...], right))
    else:
        crit = jnp.where(next_lower, right, left)
        rest = jnp.where(next_lower, left, right)
        if split:
            value, keep, send = refs
            half = crit.shape[1] // 2
            for i, side in enumerate((crit, rest)):
                keep[i] = jnp.where(next_lower, side[:, :half], side[:, half:])
                send[i] = jnp.where(next_lower, side[:, half:], side[:, :half])
        else:
            value, out = refs
            out[0] = crit
            out[1] = rest
    value[...] = product3(inverse[...], g)
    if final:
        outer[...] = product3(end[...], right)


def root_inverse(flags, crit, mine, other, out, packed):
    gather_packed(packed, mine, other, flags[0])
    (inverse,) = inverses([unpack(crit[...] + packed[...])])
    out[...] = inverse


def descend(flags, *refs, levels):
    root, own, received, far, outer = refs[:5]
    count = levels - 1
    backs, values = refs[5 : 5 + count], refs[5 + count : 5 + 2 * count]
    send, keep, send_near = refs[-3:]
    lower = flags[2 + levels - 1] == 0
    q = product3(root[...], own[...] + received[...])
    outer = outer[...] - product3(far[...], q, TN)
    p = jnp.where(lower, 0.0, q)
    r = jnp.where(lower, q, outer)
    for level in range(levels - 2, -1, -1):
        if level:
            value = values[level][...]
        else:
            half = keep.shape[2]
            value = values[level][:, pl.ds(pl.multiple_of(flags[3] * half, half), half)]
        q = value - product3(backs[level][0], p) - product3(backs[level][1], r)
        lower = flags[2 + level] == 0
        if level == 1:
            send[0] = jnp.where(lower, q, p)
            send[1] = jnp.where(lower, r, q)
        if level == 0:
            send_near[0] = jnp.where(lower, q, p)
            send_near[1] = jnp.where(lower, r, q)
        p, r = jnp.where(lower, p, q), jnp.where(lower, q, r)
    keep[0] = p
    keep[1] = r


def descend_last(flags, mine, back, value, keep, send):
    half = keep.shape[2]
    place = 1 - flags[3]
    p, r = mine[0], mine[1]
    q = value[:, pl.ds(pl.multiple_of(place * half, half), half)] - product3(back[0], p) - product3(back[1], r)
    lower = flags[2] == 0
    keep[0] = jnp.where(lower, p, q)
    keep[1] = jnp.where(lower, q, r)
    send[0] = jnp.where(lower, q, p)
    send[1] = jnp.where(lower, r, q)


def finish(flags, keep, received, spikes, interior, *refs, width, classes, own):
    out, ends, rows, sems = refs[-4:]
    quarter = classes // 4
    place = flags[3] if own else 1 - flags[3]
    columns = [pl.ds(pl.multiple_of(k * 2 * quarter + place * quarter, quarter), quarter) for k in range(2)]
    lower = flags[0] == 0
    copies = []

    def leave(source, block):
        for k in range(2):
            copies.append(
                pltpu.make_async_copy(
                    source.at[:, pl.ds(k * quarter, quarter)],
                    out.at[pl.ds(block * width, width), columns[k]],
                    sems.at[2 * block + k],
                )
            )
            copies[-1].start()

    for i in range(2):
        ends[i * width : (i + 1) * width, :quarter] = jnp.where(lower, keep[i], received[i])
        ends[i * width : (i + 1) * width, quarter:] = jnp.where(lower, received[i], keep[i])
    leave(ends.at[pl.ds(width, width)], 3)
    for i in range(3):
        side = jnp.concatenate([interior[i, :, columns[0]], interior[i, :, columns[1]]], axis=1)
        rows[i] = side - product3(spikes[i], ends[...])
        leave(rows.at[i], i)
    for copy in copies:
        copy.wait()


def swapped(array, distance):
    length = lax.axis_size("slab")
    return lax.ppermute(array, "slab", [(i, i ^ distance) for i in range(length)])


def shards(diag_tiles, coupling, labels, confidence):
    blocks, width, _ = diag_tiles.shape
    classes = C
    square, pair = (width, width), (2, width, width)
    packed, message = (width // 2 + 8, width), (width // 2 + width // 4 + 8, width)
    wide, narrow = (width, classes // 2), (width, classes // 4)
    levels = lax.axis_size("slab").bit_length() - 1
    position = lax.axis_index("slab")
    flags = jnp.stack([position & 1, (position == 0).astype(jnp.int32)] + [(position >> k) & 1 for k in range(levels)])
    seeds = jnp.concatenate([labels.reshape(blocks, width).astype(f32), confidence.reshape(blocks, width)], axis=0)
    diag_tiles = pltpu.with_memory_space_constraint(diag_tiles, pltpu.HBM)
    coupling = pltpu.with_memory_space_constraint(coupling, pltpu.HBM)
    inverse, link, crit, rest = call(
        functools.partial(local_factor, width=width),
        [(3,) + square, (6,) + square, square, pair],
        [flags, diag_tiles, coupling],
        13,
        [(4,) + square, (4,) + square, (3,) + square, pltpu.SemaphoreType.DMA((11,))],
        (1, 2),
        (0,),
    )
    received_crit = swapped(crit, 1)
    received_rest = [swapped(rest, 1)]
    sides, send, inner = call(
        functools.partial(local_sides, width=width, classes=classes),
        [(2,) + wide, (2,) + wide, (3, width, classes)],
        [flags, seeds, link],
        3,
    )
    received_crit, send = lax.optimization_barrier((received_crit, send))
    received_sides = swapped(send, 1)
    backs, values = [], []
    for level in range(levels - 1):
        final = level == levels - 2
        halved = level > 0
        (middle,) = call(
            functools.partial(level_inverse, packed=halved), [square], [flags, crit, received_crit], 4.5
        )
        if halved:
            arrived, middle = lax.optimization_barrier((received_rest, middle))
            received_rest = [arrived, swapped(arrived, 1)]
            if final:
                send, middle = lax.optimization_barrier((send, middle))
        if final:
            back, crit, end, far, message = call(
                functools.partial(level_end, level=level),
                [pair, packed, square, square, (width // 4 + 8, width)],
                [flags, middle, rest] + received_rest,
                7,
                [pair],
            )
            received_crit = swapped(message, 2 ** (level + 1))
        else:
            crit, scaled, *joined = call(
                functools.partial(level_crit, halved=halved, level=level),
                [packed, square] + [pair] * halved,
                [flags, middle, rest] + received_rest,
                1.2,
            )
            if halved:
                crit, send = lax.optimization_barrier((crit, send))
            received_crit = swapped(crit, 2 ** (level + 1))
            back, rest, rest_half = call(
                functools.partial(level_rest, level=level),
                [pair, pair, message],
                [flags, middle, scaled, rest] + (joined or received_rest),
                1.2,
                [packed],
            )
            received_rest = swapped(rest_half, 2 ** (level + 1))
        if halved:
            received_sides = swapped(send, 2**level)
        split = level == 0
        columns = wide if split else narrow
        value, *others = call(
            functools.partial(level_sides, level=level, split=split, final=final),
            [columns] + ([columns, columns] if final else [(2,) + narrow, (2,) + narrow] if split else [(2,) + columns]),
            [flags, middle, back, sides, received_sides] + ([far, end] if final else []),
            0.05 if final else 1,
        )
        if final:
            own, outer = others
            own, inner = lax.optimization_barrier((own, inner))
            spikes, interior = call(
                functools.partial(local_spikes, width=width),
                [(3, width, 2 * width), (3, width, classes)],
                [flags, inverse, link, inner],
                0.05,
                [(3,) + square, pltpu.SemaphoreType.DMA(())],
                (1,),
            )
            received_crit, spikes, interior = lax.optimization_barrier((received_crit, spikes, interior))
            received_own = swapped(own, 2 ** (level + 1))
        else:
            sides, send = others[0], others[-1]
        backs.append(back)
        values.append(value)
    (root,) = call(root_inverse, [square], [flags, crit, received_crit, swapped(received_crit, 1)], 0.05, [packed])
    send, keep, send_near = call(
        functools.partial(descend, levels=levels),
        [(2,) + narrow, (2,) + narrow, (2,) + narrow],
        [flags, root, own, received_own, far, outer] + backs + values,
        2,
    )
    arrived = swapped(send, 2)
    near = swapped(send_near, 1)
    out = []
    for own in (True, False):
        out = call(
            functools.partial(finish, width=width, classes=classes, own=own),
            [(blocks * width, classes)],
            [flags, keep, near, spikes, interior, *out],
            0.05 if own else 2,
            [(2 * width, classes // 2), (3, width, classes // 2), pltpu.SemaphoreType.DMA((8,))],
            () if own else (5,),
            (0,),
            {} if own else {5: 0},
        )
        if own:
            arrived, *out = lax.optimization_barrier((arrived, *out))
            keep, send = call(
                descend_last, [(2,) + narrow, (2,) + narrow], [flags, arrived, backs[0], values[0]], 0.7
            )
            near = swapped(send, 1)
    (out,) = out
    return out


def solution(mesh):
    in_specs = (P("slab", None, None), P("slab", None, None), P("slab"), P("slab"))
    out_specs = P("slab", None)
    return jax.shard_map(shards, mesh=mesh, in_specs=in_specs, out_specs=out_specs, check_vma=False)
```

```python
import functools

import jax
import jax.numpy as jnp
from jax import lax
from jax.experimental import pallas as pl
from jax.experimental.pallas import tpu as pltpu
from jax.sharding import PartitionSpec as P

C = 512

alpha_rate = 0.995

f32 = jnp.float32
bf16 = jnp.bfloat16

NN = (((1,), (0,)), ((), ()))
NT = (((1,), (1,)), ((), ()))
TN = (((0,), (0,)), ((), ()))


def product(left, right, dims=NN):
    return lax.dot_general(left, right, dims, precision=lax.Precision.HIGHEST, preferred_element_type=f32)


def single(left, right, dims=NN):
    return lax.dot_general(left, right, dims, preferred_element_type=f32)


def halves(array):
    high = array.astype(bf16)
    return high, (array - high.astype(f32)).astype(bf16)


def product3(left, right, dims=NN):
    left_high, left_low = halves(left)
    right_high, right_low = halves(right)
    return single(left_high, right_high, dims) + (
        single(left_high, right_low, dims) + single(left_low, right_high, dims)
    )


def narrow_product(left, right):
    return single(left.astype(bf16), right.astype(bf16))


def unit(width):
    rows = lax.broadcasted_iota(jnp.int32, (width, width), 0)
    columns = lax.broadcasted_iota(jnp.int32, (width, width), 1)
    return (rows == columns).astype(f32)


DOUBLINGS = 6


def inverses(matrices):
    width = matrices[0].shape[0]
    identity = unit(width)
    scale = 1.0 / alpha_rate
    residuals = [identity - matrix for matrix in matrices]
    results = [identity for _ in matrices]
    for step in range(DOUBLINGS):
        following = 2.0 * scale * scale - 1.0
        gain = 2.0 * scale * scale / following
        for i, (residual, result) in enumerate(zip(residuals, results)):
            high, low = halves(residual)
            both = jnp.concatenate([high, low], axis=1)

            def times(left_high, left_low):
                wide = single(left_high, both)
                return wide[:, :width] + (wide[:, width:] + single(left_low, high))

            if step < DOUBLINGS - 1:
                residuals[i] = gain * times(high, low) - identity * (1.0 / following)
            results[i] = gain * (result + (times(*halves(result)) if step else residual))
        scale = following
    errors = [identity - product(matrix, result) for matrix, result in zip(matrices, results)]
    squares = [narrow_product(error, error) for error in errors]
    cubes = [narrow_product(error, square) for error, square in zip(errors, squares)]
    return [
        result + product3(result, error + (square + cube))
        for result, error, square, cube in zip(results, errors, squares, cubes)
    ]


def call(kernel, shapes, operands, microseconds, scratch=(), hbm=(), out_hbm=(), alias={}):
    in_specs = [pl.BlockSpec(memory_space=pltpu.VMEM) for _ in operands]
    in_specs[0] = pl.BlockSpec(memory_space=pltpu.SMEM)
    for index in hbm:
        in_specs[index] = pl.BlockSpec(memory_space=pltpu.HBM)
    return pl.pallas_call(
        kernel,
        out_shape=[pltpu.HBM(s, f32) if i in out_hbm else jax.ShapeDtypeStruct(s, f32) for i, s in enumerate(shapes)],
        in_specs=in_specs,
        out_specs=[pl.BlockSpec(memory_space=pltpu.HBM if i in out_hbm else pltpu.VMEM) for i in range(len(shapes))],
        input_output_aliases=alias,
        scratch_shapes=[pltpu.VMEM(shape, f32) if isinstance(shape, tuple) else shape for shape in scratch],
        cost_estimate=pl.CostEstimate(flops=int(microseconds * 1.1e9), bytes_accessed=0, transcendentals=0),
        compiler_params=pltpu.CompilerParams(vmem_limit_bytes=12 * 2**20),
    )(*operands)


def join_rows(target, mine, other, core):
    half = mine.shape[-2]
    target[..., pl.ds(pl.multiple_of(core * half, half), half), :] = mine[...]
    target[..., pl.ds(pl.multiple_of((1 - core) * half, half), half), :] = other[...]


def pack(matrix, out):
    half = matrix.shape[0] // 2
    rows = lax.broadcasted_iota(jnp.int32, (half, half), 0)
    columns = lax.broadcasted_iota(jnp.int32, (half, half), 1)
    last = matrix[half:, half:]
    out[:half, :half] = matrix[half:, :half]
    out[:half, half:] = jnp.where(rows >= columns, matrix[:half, :half], last)
    diagonal = jnp.sum(jnp.where(rows == columns, last, 0.0), axis=0, keepdims=True)
    out[half:, half:] = jnp.broadcast_to(diagonal, (8, half))
    out[half:, :half] = jnp.zeros((8, half), f32)


def unpack(packed):
    half = packed.shape[1] // 2
    rows = lax.broadcasted_iota(jnp.int32, (half, half), 0)
    columns = lax.broadcasted_iota(jnp.int32, (half, half), 1)
    corner = packed[:half, :half]
    both = packed[:half, half:]
    flipped = both.T
    diagonal = packed[half : half + 1, half:]
    first = jnp.where(rows >= columns, both, flipped)
    last = jnp.where(rows < columns, both, jnp.where(rows > columns, flipped, diagonal))
    return jnp.concatenate(
        [jnp.concatenate([first, corner.T], axis=1), jnp.concatenate([corner, last], axis=1)], axis=0
    )


def local_factor(flags, diag_in, coupling_in, inverse_out, link_out, crit, rest, diag, coupling, inner, sems, *, width):
    copies = []
    for i in (0, 2, 1, 3):
        copies.append(pltpu.make_async_copy(diag_in.at[i], diag.at[i], sems.at[i]))
    for i in range(4):
        copies.append(pltpu.make_async_copy(coupling_in.at[i], coupling.at[i], sems.at[4 + i]))
    for copy in copies:
        copy.start()
    identity = unit(width)
    copies[0].wait()
    copies[1].wait()
    v0, v2 = inverses([identity - alpha_rate * diag[0], identity - alpha_rate * diag[2]])
    for copy in copies[2:]:
        copy.wait()
    inner[0] = v0
    inner[2] = v2
    copies = [pltpu.make_async_copy(inner.at[i], inverse_out.at[i], sems.at[8 + i]) for i in range(3)]
    copies[0].start()
    copies[2].start()
    d1 = identity - alpha_rate * diag[1]
    d3 = identity - alpha_rate * diag[3]
    l = [-alpha_rate * coupling[i] for i in range(4)]
    l[0] = jnp.where(flags[1] == 1, 0.0, l[0])
    v0_l1t = product3(v0, l[1], NT)
    v2_l2 = product3(v2, l[2])
    middle = d1 - product3(l[1], v0_l1t) - product3(l[2], v2_l2, TN)
    (v1,) = inverses([middle])
    inner[1] = v1
    copies[1].start()
    v0_l0 = product3(v0, l[0])
    v2_l3t = product3(v2, l[3], NT)
    g = -product3(l[1], v0_l0)
    h = -product3(l[2], v2_l3t, TN)
    v1_g = product3(v1, g)
    v1_h = product3(v1, h)
    left = -product3(l[0], v0_l0, TN) - product3(g, v1_g, TN)
    right = d3 - product3(l[3], v2_l3t) - product3(h, v1_h, TN)
    across = -product3(g, v1_h, TN)
    crit[...] = jnp.where(flags[2] == 0, right, left)
    rest[0] = jnp.where(flags[2] == 0, left, right)
    rest[1] = across
    for i, value in enumerate((v0_l0, v0_l1t, v1_g, v1_h, v2_l2, v2_l3t)):
        link_out[i] = value
    for copy in copies:
        copy.wait()


def local_sides(flags, seeds, link, keep, send, interior, *, width, classes):
    place = lax.broadcasted_iota(jnp.int32, (width, classes), 1).astype(f32)
    turned = seeds[...].T
    b = [jnp.where(turned[:, i : i + 1] == place, turned[:, 4 + i : 5 + i], 0.0) for i in range(4)]

    def from_seeds(index, i):
        chosen = jnp.where(turned[:, i : i + 1] == place, 1.0, 0.0).astype(bf16)
        high, low = halves(link[index] * turned[:, 4 + i : 5 + i])
        return single(high, chosen, TN) + single(low, chosen, TN)

    b1 = b[1] - from_seeds(1, 0) - from_seeds(4, 2)
    left = -from_seeds(0, 0) - product3(link[2], b1, TN)
    right = b[3] - from_seeds(5, 2) - product3(link[3], b1, TN)
    interior[0] = b[0]
    interior[1] = b1
    interior[2] = b[2]
    lower = flags[0] == 0
    half = classes // 2
    crit = jnp.where(lower, right, left)
    rest = jnp.where(lower, left, right)
    keep[0] = jnp.where(lower, crit[:, :half], crit[:, half:])
    keep[1] = jnp.where(lower, rest[:, :half], rest[:, half:])
    send[0] = jnp.where(lower, crit[:, half:], crit[:, :half])
    send[1] = jnp.where(lower, rest[:, half:], rest[:, :half])


def local_spikes(flags, inverse_in, link, sides, spikes, interior, inverse, sem, *, width):
    copy = pltpu.make_async_copy(inverse_in, inverse, sem)
    copy.start()
    s1 = jnp.concatenate([link[2], link[3]], axis=1)
    spikes[1] = s1
    first = -product3(link[1], s1)
    spikes[0, :, :width] = first[:, :width] + link[0]
    spikes[0, :, width:] = first[:, width:]
    last = -product3(link[4], s1)
    spikes[2, :, :width] = last[:, :width]
    spikes[2, :, width:] = last[:, width:] + link[5]
    copy.wait()
    y1 = product3(inverse[1], sides[1])
    interior[1] = y1
    interior[0] = product3(inverse[0], sides[0]) - product3(link[1], y1)
    interior[2] = product3(inverse[2], sides[2]) - product3(link[4], y1)


def level_inverse(flags, crit, received, out, *, packed):
    total = crit[...] + received[...]
    (inverse,) = inverses([unpack(total) if packed else total])
    out[...] = inverse


def gather_packed(packed, mine, other, core):
    rows = mine.shape[0] - 8
    packed[pl.ds(pl.multiple_of(core * rows, 8), rows + 8), :] = mine[...]
    packed[pl.ds(pl.multiple_of((1 - core) * rows, 8), rows + 8), :] = other[...]


def gather_rest(whole, mine, other, core):
    half = whole.shape[1] // 2
    join_rows(whole.at[1], mine.at[:half], other.at[:half], core)
    gather_packed(whole.at[0], mine.at[half:], other.at[half:], core)
    whole[0] = unpack(whole[0, : half + 8, :])


def level_crit(flags, inverse, rest, received, *refs, halved, level):
    if halved:
        other, crit_out, scaled_out, whole = refs
        gather_rest(whole, received, other, flags[0])
        received = whole
    else:
        crit_out, scaled_out = refs
    lower = flags[2 + level] == 0
    next_lower = flags[3 + level] == 0
    from_received = lower == next_lower
    base = jnp.where(from_received, received[0], rest[0])
    link = jnp.where(from_received, received[1], rest[1])
    link = jnp.where(next_lower, link, link.T)
    scaled = product3(inverse[...], link)
    scaled_out[...] = scaled
    pack(base - product3(link, scaled, TN), crit_out)


def level_rest(flags, inverse, scaled, rest, received, back, rest_out, message, packed, *, level):
    lower = flags[2 + level] == 0
    next_lower = flags[3 + level] == 0
    from_received = lower == next_lower
    base = jnp.where(from_received, rest[0], received[0])
    link = jnp.where(from_received, rest[1], received[1])
    near = jnp.where(from_received, received[1], rest[1])
    link = jnp.where(next_lower, link.T, link)
    other = product3(inverse[...], link)
    matrix = base - product3(link, other, TN)
    rest_out[0] = matrix
    to_left = jnp.where(next_lower, other, scaled[...])
    to_right = jnp.where(next_lower, scaled[...], other)
    back[0] = to_left
    back[1] = to_right
    rest_out[1] = -product3(jnp.where(next_lower, link.T, near), to_right)
    half = matrix.shape[0] // 2
    message[:half, :] = rest_out[1, pl.ds(pl.multiple_of(flags[0] * half, half), half), :]
    pack(matrix, packed)
    rows = half // 2
    message[half:, :] = packed[pl.ds(pl.multiple_of(flags[0] * rows, 8), rows + 8), :]


def level_end(flags, inverse, rest, received, other, back, crit_out, end, far, message, whole, *, level):
    gather_rest(whole, received, other, flags[0])
    received = whole
    lower = flags[2 + level] == 0
    a_left = jnp.where(lower, rest[0], received[0])
    b_left = jnp.where(lower, rest[1], received[1])
    c_right = jnp.where(lower, received[0], rest[0])
    b_right = jnp.where(lower, received[1], rest[1])
    to_left = product3(inverse[...], b_left, NT)
    to_right = product3(inverse[...], b_right)
    left = a_left - product3(b_left, to_left)
    right = c_right - product3(b_right, to_right, TN)
    across = -product3(b_left, to_right)
    back[0] = to_left
    back[1] = to_right
    (last,) = inverses([right])
    end[...] = last
    scaled = product3(across, last)
    far[...] = scaled
    pack(jnp.where(flags[3 + level] == 0, right, left - product3(scaled, across, NT)), crit_out)
    rows = message.shape[0] - 8
    message[...] = crit_out[pl.ds(pl.multiple_of(flags[0] * rows, 8), rows + 8), :]


def level_sides(flags, inverse, back, own, received, *refs, level, split, final):
    lower = flags[2 + level] == 0
    g = own[0] + received[0]
    a_left = jnp.where(lower, own[1], received[1])
    c_right = jnp.where(lower, received[1], own[1])
    left = a_left - product3(back[0], g, TN)
    right = c_right - product3(back[1], g, TN)
    next_lower = flags[3 + level] == 0
    if final:
        far, end, value, out, outer = refs
        out[...] = jnp.where(next_lower, right, left - product3(far[...], right))
    else:
        crit = jnp.where(next_lower, right, left)
        rest = jnp.where(next_lower, left, right)
        if split:
            value, keep, send = refs
            half = crit.shape[1] // 2
            for i, side in enumerate((crit, rest)):
                keep[i] = jnp.where(next_lower, side[:, :half], side[:, half:])
                send[i] = jnp.where(next_lower, side[:, half:], side[:, :half])
        else:
            value, out = refs
            out[0] = crit
            out[1] = rest
    value[...] = product3(inverse[...], g)
    if final:
        outer[...] = product3(end[...], right)


def root_inverse(flags, crit, mine, other, out, packed):
    gather_packed(packed, mine, other, flags[0])
    (inverse,) = inverses([unpack(crit[...] + packed[...])])
    out[...] = inverse


def descend(flags, *refs, levels):
    root, own, received, far, outer = refs[:5]
    count = levels - 1
    backs, values = refs[5 : 5 + count], refs[5 + count : 5 + 2 * count]
    send, keep, send_near = refs[-3:]
    lower = flags[2 + levels - 1] == 0
    q = product3(root[...], own[...] + received[...])
    outer = outer[...] - product3(far[...], q, TN)
    p = jnp.where(lower, 0.0, q)
    r = jnp.where(lower, q, outer)
    for level in range(levels - 2, -1, -1):
        if level:
            value = values[level][...]
        else:
            half = keep.shape[2]
            value = values[level][:, pl.ds(pl.multiple_of(flags[3] * half, half), half)]
        q = value - product3(backs[level][0], p) - product3(backs[level][1], r)
        lower = flags[2 + level] == 0
        if level == 1:
            send[0] = jnp.where(lower, q, p)
            send[1] = jnp.where(lower, r, q)
        if level == 0:
            send_near[0] = jnp.where(lower, q, p)
            send_near[1] = jnp.where(lower, r, q)
        p, r = jnp.where(lower, p, q), jnp.where(lower, q, r)
    keep[0] = p
    keep[1] = r


def descend_last(flags, mine, back, value, keep, send):
    half = keep.shape[2]
    place = 1 - flags[3]
    p, r = mine[0], mine[1]
    q = value[:, pl.ds(pl.multiple_of(place * half, half), half)] - product3(back[0], p) - product3(back[1], r)
    lower = flags[2] == 0
    keep[0] = jnp.where(lower, p, q)
    keep[1] = jnp.where(lower, q, r)
    send[0] = jnp.where(lower, q, p)
    send[1] = jnp.where(lower, r, q)


def finish(flags, keep, received, spikes, interior, *refs, width, classes, own):
    out, ends, rows, sems = refs[-4:]
    quarter = classes // 4
    place = flags[3] if own else 1 - flags[3]
    columns = [pl.ds(pl.multiple_of(k * 2 * quarter + place * quarter, quarter), quarter) for k in range(2)]
    lower = flags[0] == 0
    copies = []

    def leave(source, block):
        for k in range(2):
            copies.append(
                pltpu.make_async_copy(
                    source.at[:, pl.ds(k * quarter, quarter)],
                    out.at[pl.ds(block * width, width), columns[k]],
                    sems.at[2 * block + k],
                )
            )
            copies[-1].start()

    for i in range(2):
        ends[i * width : (i + 1) * width, :quarter] = jnp.where(lower, keep[i], received[i])
        ends[i * width : (i + 1) * width, quarter:] = jnp.where(lower, received[i], keep[i])
    leave(ends.at[pl.ds(width, width)], 3)
    for i in range(3):
        side = jnp.concatenate([interior[i, :, columns[0]], interior[i, :, columns[1]]], axis=1)
        rows[i] = side - product3(spikes[i], ends[...])
        leave(rows.at[i], i)
    for copy in copies:
        copy.wait()


def swapped(array, distance):
    length = lax.axis_size("slab")
    return lax.ppermute(array, "slab", [(i, i ^ distance) for i in range(length)])


def shards(diag_tiles, coupling, labels, confidence):
    blocks, width, _ = diag_tiles.shape
    classes = C
    square, pair = (width, width), (2, width, width)
    packed, message = (width // 2 + 8, width), (width // 2 + width // 4 + 8, width)
    wide, narrow = (width, classes // 2), (width, classes // 4)
    levels = lax.axis_size("slab").bit_length() - 1
    position = lax.axis_index("slab")
    flags = jnp.stack([position & 1, (position == 0).astype(jnp.int32)] + [(position >> k) & 1 for k in range(levels)])
    seeds = jnp.concatenate([labels.reshape(blocks, width).astype(f32), confidence.reshape(blocks, width)], axis=0)
    diag_tiles = pltpu.with_memory_space_constraint(diag_tiles, pltpu.HBM)
    coupling = pltpu.with_memory_space_constraint(coupling, pltpu.HBM)
    inverse, link, crit, rest = call(
        functools.partial(local_factor, width=width),
        [(3,) + square, (6,) + square, square, pair],
        [flags, diag_tiles, coupling],
        13,
        [(4,) + square, (4,) + square, (3,) + square, pltpu.SemaphoreType.DMA((11,))],
        (1, 2),
        (0,),
    )
    received_crit = swapped(crit, 1)
    received_rest = [swapped(rest, 1)]
    backs, values = [], []
    for level in range(levels - 1):
        final = level == levels - 2
        halved = level > 0
        (middle,) = call(
            functools.partial(level_inverse, packed=halved), [square], [flags, crit, received_crit], 4.5
        )
        if halved:
            arrived, middle = lax.optimization_barrier((received_rest, middle))
            received_rest = [arrived, swapped(arrived, 1)]
            if final:
                send, middle = lax.optimization_barrier((send, middle))
        if final:
            back, crit, end, far, message = call(
                functools.partial(level_end, level=level),
                [pair, packed, square, square, (width // 4 + 8, width)],
                [flags, middle, rest] + received_rest,
                7,
                [pair],
            )
            received_crit = swapped(message, 2 ** (level + 1))
        else:
            crit, scaled, *joined = call(
                functools.partial(level_crit, halved=halved, level=level),
                [packed, square] + [pair] * halved,
                [flags, middle, rest] + received_rest,
                1.2,
            )
            if halved:
                crit, send = lax.optimization_barrier((crit, send))
            received_crit = swapped(crit, 2 ** (level + 1))
            back, rest, rest_half = call(
                functools.partial(level_rest, level=level),
                [pair, pair, message],
                [flags, middle, scaled, rest] + (joined or received_rest),
                1.2,
                [packed],
            )
            if level == 0:
                rest_half, seeds = lax.optimization_barrier((rest_half, seeds))
                sides, send, inner = call(
                    functools.partial(local_sides, width=width, classes=classes),
                    [(2,) + wide, (2,) + wide, (3, width, classes)],
                    [flags, seeds, link],
                    0.05,
                )
                received_sides = swapped(send, 1)
            received_rest = swapped(rest_half, 2 ** (level + 1))
        if halved:
            received_sides = swapped(send, 2**level)
        split = level == 0
        columns = wide if split else narrow
        value, *others = call(
            functools.partial(level_sides, level=level, split=split, final=final),
            [columns] + ([columns, columns] if final else [(2,) + narrow, (2,) + narrow] if split else [(2,) + columns]),
            [flags, middle, back, sides, received_sides] + ([far, end] if final else []),
            0.05 if final else 1,
        )
        if final:
            own, outer = others
            own, inner = lax.optimization_barrier((own, inner))
            spikes, interior = call(
                functools.partial(local_spikes, width=width),
                [(3, width, 2 * width), (3, width, classes)],
                [flags, inverse, link, inner],
                0.05,
                [(3,) + square, pltpu.SemaphoreType.DMA(())],
                (1,),
            )
            received_crit, spikes, interior = lax.optimization_barrier((received_crit, spikes, interior))
            received_own = swapped(own, 2 ** (level + 1))
        else:
            sides, send = others[0], others[-1]
        backs.append(back)
        values.append(value)
    (root,) = call(root_inverse, [square], [flags, crit, received_crit, swapped(received_crit, 1)], 0.05, [packed])
    send, keep, send_near = call(
        functools.partial(descend, levels=levels),
        [(2,) + narrow, (2,) + narrow, (2,) + narrow],
        [flags, root, own, received_own, far, outer] + backs + values,
        2,
    )
    arrived = swapped(send, 2)
    near = swapped(send_near, 1)
    out = []
    for own in (True, False):
        out = call(
            functools.partial(finish, width=width, classes=classes, own=own),
            [(blocks * width, classes)],
            [flags, keep, near, spikes, interior, *out],
            0.05 if own else 2,
            [(2 * width, classes // 2), (3, width, classes // 2), pltpu.SemaphoreType.DMA((8,))],
            () if own else (5,),
            (0,),
            {} if own else {5: 0},
        )
        if own:
            arrived, *out = lax.optimization_barrier((arrived, *out))
            keep, send = call(
                descend_last, [(2,) + narrow, (2,) + narrow], [flags, arrived, backs[0], values[0]], 0.7
            )
            near = swapped(send, 1)
    (out,) = out
    return out


def solution(mesh):
    in_specs = (P("slab", None, None), P("slab", None, None), P("slab"), P("slab"))
    out_specs = P("slab", None)
    return jax.shard_map(shards, mesh=mesh, in_specs=in_specs, out_specs=out_specs, check_vma=False)
```
